512 devices in a mesh: head: 8 (over x, core), seq: 64 (over y, z).
Axes of the slice: x: 4, y: 4, z: 16, core: 2. Of those that a mesh axis runs over, the one named last changes fastest.
Arguments:
- tokens: bfloat16 [49152, 3200], P('seq'), may hold values from -6 to 6
- ln_gain: float32 [3200], replicated, may hold values from 0.5 to 2
- w_query: bfloat16 [3200, 2048], P('seq', 'head')
- w_key: bfloat16 [3200, 2048], P('seq', 'head')
- w_value: bfloat16 [3200, 2048], P('seq', 'head'), may hold values from -0.109375 to 0.109375
- q_gain: float32 [2048], P('head'), may hold values from 0.5 to 8
- k_gain: float32 [2048], P('head'), may hold values from 0.5 to 8
- seg_ids: int32 [49152], P('seq'), may hold values from 0 to 94, never falling along the last dimension, each value on 1 to 1025 neighbouring positions
Outputs:
- attended: bfloat16 [49152, 2048], P('seq', 'head')
The draws below stay inside these ranges and needn't reach their ends.
Inputs may be any that keep to these rules, and one draw needn't show every extreme that they name: `seg_ids`: ids never fall along the tokens; each id covers 1 to 1025 consecutive tokens and one covers exactly 1025.
All inputs are finite; a program needn't handle non-finite values.
Results may differ from the reference program's by a relative error of at most 0.0055.
The reference program's roundings to bfloat16 on the way (of `normed`, `q_hat` and `weights`) count: a program that leaves them out, or rounds other values in their place, can miss the bound.
Values may be sent and summed in bfloat16 or wider, within the bound.
No kernel may reach another device: no remote copies, remote signals or barrier semaphores. Data moves between devices by JAX's collectives and lax.ppermute only.
A program may use at most 64 MiB of HBM per device.

```python
import math
import jax
import jax.numpy as jnp
import numpy as np
from jax import lax

D = 3200
HEADS = 16
HEAD_DIM = 128
MOST = 1025
TOK_DEV = 768
TOKENS = 49152
CHANNELS = 2048
SEGS = 95
N_SEQ = 64


def projection_draw(key, salt):
    own_key = jax.random.fold_in(key, salt)
    columns = HEADS * HEAD_DIM
    base = jnp.clip(jax.random.normal(own_key, (D, columns), jnp.float32), -6.0, 6.0)
    head_of = (jnp.arange(columns) // HEAD_DIM).astype(jnp.float32)
    scaled = 3.0 ** (head_of / max(HEADS - 1, 1)) / math.sqrt(D)
    return base * scaled[None, :]


def gain_draw(key, salt):
    own_key = jax.random.fold_in(key, salt)
    columns = HEADS * HEAD_DIM
    logs = jax.random.uniform(own_key, (columns,), jnp.float32, math.log(0.5), math.log(2.5))
    return jnp.exp(logs)


def draw_w_query(key, part):
    return projection_draw(key, 11).astype(jnp.bfloat16)


def draw_w_key(key, part):
    return projection_draw(key, 12).astype(jnp.bfloat16)


def draw_q_gain(key, part):
    return gain_draw(key, 21)


def draw_k_gain(key, part):
    return gain_draw(key, 22)


def steps_of(rng, extent, split, smallest, largest):
    def one(dim, parts):
        draws = jax.random.uniform(jax.random.fold_in(jax.random.fold_in(rng, 6), dim), (parts,), jnp.float32, smallest / len(split), largest / len(split))
        return jnp.repeat(jnp.exp(draws), extent[dim] // parts).reshape((-1,) + (1,) * (len(extent) - dim - 1))

    level = one(*split[0])
    for cut in split[1:]:
        level = level * one(*cut)
    return level


def length_profile(count, total, bound, skew):
    loads = [(1 << 20) // math.isqrt(standing ** skew) + 1 for standing in range(2, count + 1)]
    surplus, counts = total - bound - (count - 1), [1] * (count - 1)
    while surplus > 0:
        candidates = [i for i in range(count - 1) if counts[i] < bound]
        pool, budget = sum([loads[i] for i in candidates]), surplus
        for i in candidates:
            more = min(bound - counts[i], max(1, budget * loads[i] // pool), surplus)
            counts[i] = counts[i] + more
            surplus = surplus - more
    return np.array([bound] + counts)


def ragged_sizes(key, count, total, limit, skew):
    if count == 2:
        one = jax.random.randint(key, (), max(1, total - limit), min(limit, total - 1) + 1)
        return jnp.stack([one, total - one])
    sizes = jnp.asarray(length_profile(count, total, limit, skew), jnp.int32)
    couples = (count - 1) // 2
    donor, receiver = sizes[1:1 + 2 * couples:2], sizes[2:2 + 2 * couples:2]
    room = jnp.minimum(donor - 1, limit - receiver)
    moved = jax.random.randint(jax.random.fold_in(key, 1), (couples,), 0, 1 << 20) % (room + 1)
    sizes = sizes.at[1:1 + 2 * couples:2].set(donor - moved).at[2:2 + 2 * couples:2].set(receiver + moved)
    return sizes[jax.random.permutation(jax.random.fold_in(key, 2), count)]


def centred(stream_key, extent, scale, bound, cuts=(), kind=jnp.bfloat16):
    loudness = steps_of(stream_key, extent, cuts, -0.22, 0.18) if cuts else 1.0
    array = jax.random.normal(stream_key, extent, jnp.float32) * scale * loudness
    return jnp.minimum(jnp.maximum(array, -bound), bound).astype(kind)


def setup_inputs(seed: int = 0) -> dict:
    key_of = jax.random.split(jax.random.key(seed), 9)
    tokens = centred(key_of[0], (TOKENS, D), 1.0, 6.0, ((0, 64),))
    ln_gain = jnp.clip(jnp.exp(jax.random.uniform(key_of[1], (D,), jnp.float32, math.log(0.5), math.log(2.0))), 0.5, 2.0)
    w_query = draw_w_query(jax.random.fold_in(key_of[8], 71), 0)
    w_key = draw_w_key(jax.random.fold_in(key_of[8], 71), 0)
    w_value = centred(key_of[4], (D, CHANNELS), D ** -0.5, 0.109375, ((0, 64), (1, 8)))
    q_gain = draw_q_gain(jax.random.fold_in(key_of[8], 71), 0)
    k_gain = draw_k_gain(jax.random.fold_in(key_of[8], 71), 0)
    seg_ids = jnp.searchsorted(jnp.cumsum(ragged_sizes(key_of[7], SEGS, TOKENS, MOST, 2)), jnp.arange(TOKENS), side="right").astype(jnp.int32)
    return dict(tokens=tokens, ln_gain=ln_gain, w_query=w_query, w_key=w_key, w_value=w_value, q_gain=q_gain, k_gain=k_gain, seg_ids=seg_ids)


EPS = 1e-06

def rms_scale(values, gain, count):
    return values * lax.rsqrt(lax.optimization_barrier(jnp.sum(values * values, axis=1, keepdims=True)) / count + EPS) * gain

def reference(tokens, ln_gain, w_query, w_key, w_value, q_gain, k_gain, seg_ids):
    floats = tokens.astype(jnp.float32)
    normed = (floats * lax.rsqrt(lax.optimization_barrier(jnp.mean(floats * floats, axis=1, keepdims=True)) + EPS) * ln_gain).astype(jnp.bfloat16)
    channels = HEADS * HEAD_DIM
    queries = jnp.dot(normed, w_query, preferred_element_type=jnp.float32)
    key_part = jnp.dot(normed, w_key, preferred_element_type=jnp.float32)
    value_part = jnp.dot(normed, w_value, preferred_element_type=jnp.float32)
    q_hat = lax.optimization_barrier(rms_scale(queries, q_gain, channels).astype(jnp.bfloat16))
    k_hat = lax.optimization_barrier(rms_scale(key_part, k_gain, channels).astype(jnp.bfloat16))
    v_hat = lax.optimization_barrier(value_part.astype(jnp.bfloat16))
    margin = MOST - 1
    keys_padded = jnp.pad(k_hat, ((margin, margin), (0, 0)))
    values_padded = jnp.pad(v_hat, ((margin, margin), (0, 0)))
    marks = (seg_ids + 1).astype(jnp.int32)
    marks_padded = jnp.pad(marks, (margin, margin))
    span = TOK_DEV + 2 * margin
    scale = 1.0 / math.sqrt(HEAD_DIM)

    def one_block(index):
        start = (index * TOK_DEV).astype(jnp.int32)
        q_block = lax.dynamic_slice_in_dim(q_hat, start, TOK_DEV, 0).astype(jnp.float32)
        k_block = lax.dynamic_slice_in_dim(keys_padded, start, span, 0).astype(jnp.float32)
        v_block = lax.dynamic_slice_in_dim(values_padded, start, span, 0).astype(jnp.float32)
        own_marks = lax.dynamic_slice_in_dim(marks, start, TOK_DEV, 0)
        near_marks = lax.dynamic_slice_in_dim(marks_padded, start, span, 0)
        q_heads = q_block.reshape(TOK_DEV, HEADS, HEAD_DIM)
        k_heads = k_block.reshape(span, HEADS, HEAD_DIM)
        v_heads = v_block.reshape(span, HEADS, HEAD_DIM)
        scores = jnp.einsum('qhd,khd->hqk', q_heads, k_heads) * scale
        allowed = own_marks[:, None] == near_marks[None, :]
        scores = jnp.where(allowed[None, :, :], scores, -1e+30)
        highest = lax.optimization_barrier(jnp.max(scores, axis=2, keepdims=True))
        expo = jnp.exp(scores - highest)
        weights = expo / lax.optimization_barrier(jnp.sum(expo, axis=2, keepdims=True))
        weights = lax.optimization_barrier(weights.astype(jnp.bfloat16)).astype(jnp.float32)
        mixed = jnp.einsum('hqk,khd->qhd', weights, v_heads)
        return mixed.reshape(TOK_DEV, channels).astype(jnp.bfloat16)
    blocks = lax.map(one_block, jnp.arange(N_SEQ, dtype=jnp.int32))
    return blocks.reshape(TOKENS, channels)
```

```python
import functools
import math

import jax
import jax.numpy as jnp
from jax import lax
from jax.experimental import pallas as pl
from jax.experimental.pallas import tpu as pltpu
from jax.sharding import PartitionSpec as P

HEADS = 16
HEAD_DIM = 128
MOST = 1025
EPS = 1e-06
NY = 4
NZ = 16
N_SEQ = NY * NZ
N_HEAD = 8
ROWS = 768
FAR = 256
WINDOW = 2 * FAR + 3 * ROWS
CHUNK = 256
Q_BLOCK = 256
NEG = -1e30

OVER_Y = [[y * NZ + z for y in range(NY)] for z in range(NZ)]
OVER_Z = [[y * NZ + z for z in range(NZ)] for y in range(NY)]


def copies_to_all(value, axis, size, groups=None):
    stacked = jnp.broadcast_to(value[None], (size,) + value.shape)
    return lax.all_to_all(stacked, axis, 0, 0, axis_index_groups=groups)


def shifted(value, by):
    pairs = [(i, i + by) for i in range(N_SEQ) if 0 <= i + by < N_SEQ]
    return lax.ppermute(value, "seq", pairs)


def halo(value):
    far = value[ROWS - FAR :]
    near = value[:FAR]
    return shifted(far, 2), shifted(value, 1), shifted(value, -1), shifted(near, -2)


def attend_kernel(
    lo_ref, hi_ref, q_ref, own_ref, near_ref, ka, kb, kc, kd, ke, va, vb, vc, vd, ve,
    out_ref, k_win, v_win, s_ref,
):
    start = 0
    for k_part, v_part in ((ka, va), (kb, vb), (kc, vc), (kd, vd), (ke, ve)):
        rows = k_part.shape[0]
        k_win[start : start + rows, :] = k_part[...]
        v_win[start : start + rows, :] = v_part[...]
        start += rows
    scale = 1.0 / math.sqrt(HEAD_DIM)
    heads_here = q_ref.shape[1] // HEAD_DIM
    for block in range(ROWS // Q_BLOCK):
        first, last = lo_ref[block], hi_ref[block]
        r0 = block * Q_BLOCK
        own = own_ref[r0 : r0 + Q_BLOCK, :]
        for head in range(heads_here):
            c0 = head * HEAD_DIM
            q = q_ref[r0 : r0 + Q_BLOCK, c0 : c0 + HEAD_DIM]

            def scores(c, top):
                k = k_win[pl.ds(c * CHUNK, CHUNK), c0 : c0 + HEAD_DIM]
                s = lax.dot_general(
                    q, k, (((1,), (1,)), ((), ())), preferred_element_type=jnp.float32
                )
                s = jnp.where(own == near_ref[c], s * scale, NEG)
                s_ref[c] = s
                for part in range(CHUNK // 128):
                    top = jnp.maximum(top, s[:, part * 128 : part * 128 + 128])
                return top

            top = lax.fori_loop(
                first, last, scores, jnp.full((Q_BLOCK, 128), NEG, jnp.float32)
            )
            highest = jnp.max(top, axis=1, keepdims=True)

            def expos(c, total):
                e = jnp.exp(s_ref[c] - highest)
                s_ref[c] = e
                for part in range(CHUNK // 128):
                    total = total + e[:, part * 128 : part * 128 + 128]
                return total

            total = lax.fori_loop(first, last, expos, jnp.zeros((Q_BLOCK, 128), jnp.float32))
            inverse = 1.0 / jnp.sum(total, axis=1, keepdims=True)

            def mix(c, acc):
                w = (s_ref[c] * inverse).astype(jnp.bfloat16)
                v = v_win[pl.ds(c * CHUNK, CHUNK), c0 : c0 + HEAD_DIM]
                return acc + jnp.dot(w, v, preferred_element_type=jnp.float32)

            acc = lax.fori_loop(first, last, mix, jnp.zeros((Q_BLOCK, HEAD_DIM), jnp.float32))
            out_ref[r0 : r0 + Q_BLOCK, c0 : c0 + HEAD_DIM] = acc.astype(jnp.bfloat16)


def attend(lo, hi, q, own, near, k_parts, v_parts):
    vmem = pl.BlockSpec(memory_space=pltpu.VMEM)
    smem = pl.BlockSpec(memory_space=pltpu.SMEM)
    width = q.shape[1]
    return pl.pallas_call(
        attend_kernel,
        out_shape=jax.ShapeDtypeStruct((ROWS, width), jnp.bfloat16),
        in_specs=[smem, smem] + [vmem] * 13,
        out_specs=vmem,
        scratch_shapes=[
            pltpu.VMEM((WINDOW, width), jnp.bfloat16),
            pltpu.VMEM((WINDOW, width), jnp.bfloat16),
            pltpu.VMEM((WINDOW // CHUNK, Q_BLOCK, CHUNK), jnp.float32),
        ],
        compiler_params=pltpu.CompilerParams(vmem_limit_bytes=32 << 20),
        cost_estimate=pl.CostEstimate(
            flops=4 * ROWS * WINDOW * width, transcendentals=ROWS * WINDOW * 2, bytes_accessed=4 << 20
        ),
        name="attend",
    )(lo, hi, q, own, near, *k_parts, *v_parts)


def on_device(tokens, ln_gain, w_query, w_key, w_value, q_gain, k_gain, seg_ids):
    total_channels = HEADS * HEAD_DIM
    width = w_query.shape[1]
    vq = copies_to_all(jnp.concatenate([w_value, w_query], axis=1), "seq", NY, OVER_Y)
    w_key, vq = lax.optimization_barrier((w_key, vq))
    vq = lax.all_gather(vq, "seq", axis=0, axis_index_groups=OVER_Z)
    k_z = lax.all_gather(w_key, "seq", axis=0, axis_index_groups=OVER_Z)
    k_all = copies_to_all(k_z, "seq", NY, OVER_Y).reshape(-1, width)

    floats = tokens.astype(jnp.float32)
    normed = (
        floats * lax.rsqrt(jnp.mean(floats * floats, axis=1, keepdims=True) + EPS) * ln_gain
    ).astype(jnp.bfloat16)
    normed = lax.optimization_barrier(normed)

    def project(rows):
        return jnp.dot(normed, rows, preferred_element_type=jnp.float32)

    def unit(values, gain):
        own = jnp.sum(values * values, axis=1)
        square = jnp.sum(copies_to_all(own, "head", N_HEAD), axis=0)
        return (values * lax.rsqrt(square[:, None] / total_channels + EPS) * gain).astype(
            jnp.bfloat16
        )

    marks = seg_ids + 1
    mark_parts = halo(marks.astype(jnp.bfloat16))
    k_hat = unit(project(k_all), k_gain)
    k_parts = halo(k_hat)

    vq = jnp.transpose(vq, (1, 0, 2, 3)).reshape(-1, 2 * width)
    v_hat = project(vq[:, :width]).astype(jnp.bfloat16)
    v_parts = halo(v_hat)
    q_hat = unit(project(vq[:, width:]), q_gain)

    near = jnp.concatenate(
        [p.astype(jnp.int32) for p in mark_parts[:2]] + [marks] + [p.astype(jnp.int32) for p in mark_parts[2:]]
    )
    blocks = marks.reshape(-1, Q_BLOCK)
    low, high = blocks[:, :1], blocks[:, -1:]
    hit = (near[None, :] >= low) & (near[None, :] <= high)
    spots = jnp.arange(WINDOW, dtype=jnp.int32)[None, :]
    lo = jnp.min(jnp.where(hit, spots, WINDOW), axis=1) // CHUNK
    hi = jnp.max(jnp.where(hit, spots, -1), axis=1) // CHUNK + 1
    return attend(
        lo,
        hi,
        q_hat,
        marks[:, None],
        near.reshape(WINDOW // CHUNK, 1, CHUNK),
        (*k_parts[:2], k_hat, *k_parts[2:]),
        (*v_parts[:2], v_hat, *v_parts[2:]),
    )


def solution(mesh):
    return jax.shard_map(
        on_device,
        mesh=mesh,
        in_specs=(
            P("seq", None),
            P(),
            P("seq", "head"),
            P("seq", "head"),
            P("seq", "head"),
            P("head"),
            P("head"),
            P("seq"),
        ),
        out_specs=P("seq", "head"),
        check_vma=False,
    )
```

```python
import math

import jax
import jax.numpy as jnp
from jax import lax
from jax.experimental import pallas as pl
from jax.experimental.pallas import tpu as pltpu
from jax.sharding import PartitionSpec as P

D = 3200
HEADS = 16
HEAD_DIM = 128
MOST = 1025
EPS = 1e-06
NX = 4
NY = 4
NZ = 16
N_SEQ = NY * NZ
N_HEAD = 8
ROWS = 768
FAR = 256
NEAR_PART = ROWS // N_HEAD
FAR_PART = FAR // N_HEAD
HALF = NEAR_PART + FAR_PART
WINDOW = 2 * FAR + 3 * ROWS
OWN = FAR + ROWS
BLOCK = 256
N_BLOCKS = WINDOW // BLOCK
Q_BLOCKS = ROWS // BLOCK
CHUNK = 256
NEG = -1e30
SHARD_ROWS = D // N_SEQ

OVER_Y = [[y * NZ + z for y in range(NY)] for z in range(NZ)]
OVER_Z = [[y * NZ + z for z in range(NZ)] for y in range(NY)]
VMEM = pl.BlockSpec(memory_space=pltpu.VMEM)
SMEM = pl.BlockSpec(memory_space=pltpu.SMEM)
ANY = pl.BlockSpec(memory_space=pl.ANY)


def copies_to_all(value, axis, size, groups=None):
    stacked = jnp.broadcast_to(value[None], (size,) + value.shape)
    return lax.all_to_all(stacked, axis, 0, 0, axis_index_groups=groups)


def shifted(value, by):
    pairs = [(i, i + by) for i in range(N_SEQ) if 0 <= i + by < N_SEQ]
    return lax.ppermute(value, "seq", pairs)


def along_x(value, by):
    pairs = [(2 * x + c, 2 * ((x + by) % NX) + c) for x in range(NX) for c in range(2)]
    return lax.ppermute(value, "head", pairs)


def other_core(value):
    return lax.ppermute(value, "head", [(i, i ^ 1) for i in range(N_HEAD)])


def norm_kernel(x_ref, gain_ref, out_ref, plain, moved):
    x = x_ref[...].astype(jnp.float32)
    mean = jnp.sum(x * x, axis=1, keepdims=True) * (1.0 / D)
    plain[...] = x * lax.rsqrt(mean + EPS) * gain_ref[...]
    for z in range(NZ):
        for y in range(NY):
            source = (y * NZ + z) * SHARD_ROWS
            target = (z * NY + y) * SHARD_ROWS
            moved[:, target : target + SHARD_ROWS] = plain[:, source : source + SHARD_ROWS]
    out_ref[...] = moved[...].astype(jnp.bfloat16)


def norm(tokens, gain):
    rows = 128
    return pl.pallas_call(
        norm_kernel,
        out_shape=jax.ShapeDtypeStruct((ROWS, D), jnp.bfloat16),
        grid=(ROWS // rows,),
        in_specs=[
            pl.BlockSpec((rows, D), lambda i: (i, 0)),
            pl.BlockSpec((1, D), lambda i: (0, 0)),
        ],
        out_specs=pl.BlockSpec((rows, D), lambda i: (i, 0)),
        scratch_shapes=[pltpu.VMEM((rows, D), jnp.float32)] * 2,
        compiler_params=pltpu.CompilerParams(vmem_limit_bytes=24 << 20),
        name="norm",
    )(tokens, gain)


def window_kernel(shards_ref, own_ref, *refs):
    parts, out_ref, sem = refs[:-2], refs[-2], refs[-1]
    copies = [pltpu.make_async_copy(own_ref, out_ref.at[pl.ds(OWN, ROWS)], sem.at[0])]

    def move(ref, at, rows, to):
        n = len(copies)
        to = pl.multiple_of(to, 32)
        copies.append(
            pltpu.make_async_copy(
                ref.at[pl.ds(at, rows)], out_ref.at[pl.ds(to, rows)], sem.at[n]
            )
        )

    for slot in range(N_HEAD):
        shard = shards_ref[slot]
        left, right = parts[2 * slot], parts[2 * slot + 1]
        move(left, 0, FAR_PART, shard * FAR_PART)
        move(left, FAR_PART, NEAR_PART, FAR + shard * NEAR_PART)
        move(right, 0, NEAR_PART, OWN + ROWS + shard * NEAR_PART)
        move(right, NEAR_PART, FAR_PART, OWN + 2 * ROWS + shard * FAR_PART)
    for copy in copies:
        copy.start()
    for copy in copies:
        copy.wait()


def window_of(shards, own, parts):
    return pl.pallas_call(
        window_kernel,
        out_shape=jax.ShapeDtypeStruct((WINDOW, D), jnp.bfloat16),
        in_specs=[SMEM] + [ANY] * (1 + len(parts)),
        out_specs=ANY,
        scratch_shapes=[pltpu.SemaphoreType.DMA((1 + 4 * N_HEAD,))],
        name="window",
    )(shards, own, *parts)


def row_squares(values):
    sums = jnp.sum(values * values, axis=1, keepdims=True)
    return jnp.transpose(jnp.broadcast_to(sums, (BLOCK, 128)))[:1]


def keys_kernel(x_ref, wq_ref, wk_ref, k_ref, ks_ref, q_ref, qs_ref):
    i = pl.program_id(0)
    x = x_ref[...]
    k = jnp.dot(x, wk_ref[...], preferred_element_type=jnp.float32)
    k_ref[...] = k
    ks_ref[0] = row_squares(k)

    @pl.when((i >= OWN // BLOCK) & (i < OWN // BLOCK + Q_BLOCKS))
    def _():
        q = jnp.dot(x, wq_ref[...], preferred_element_type=jnp.float32)
        q_ref[...] = q
        qs_ref[0] = row_squares(q)


def q_step(i):
    return jnp.clip(i - OWN // BLOCK, 0, Q_BLOCKS - 1)


def project_keys(window, w_all, width):
    return pl.pallas_call(
        keys_kernel,
        out_shape=(
            jax.ShapeDtypeStruct((WINDOW, width), jnp.float32),
            jax.ShapeDtypeStruct((N_BLOCKS, 1, BLOCK), jnp.float32),
            jax.ShapeDtypeStruct((ROWS, width), jnp.float32),
            jax.ShapeDtypeStruct((Q_BLOCKS, 1, BLOCK), jnp.float32),
        ),
        grid=(N_BLOCKS,),
        in_specs=[
            pl.BlockSpec((BLOCK, D), lambda i: (i, 0)),
            pl.BlockSpec((D, width), lambda i: (0, 0)),
            pl.BlockSpec((D, width), lambda i: (0, 1)),
        ],
        out_specs=(
            pl.BlockSpec((BLOCK, width), lambda i: (i, 0)),
            pl.BlockSpec((1, 1, BLOCK), lambda i: (i, 0, 0)),
            pl.BlockSpec((BLOCK, width), lambda i: (q_step(i), 0)),
            pl.BlockSpec((1, 1, BLOCK), lambda i: (q_step(i), 0, 0)),
        ),
        compiler_params=pltpu.CompilerParams(vmem_limit_bytes=32 << 20),
        name="keys",
    )(window, w_all, w_all)


def values_kernel(x_ref, w_ref, v_ref):
    v_ref[...] = jnp.dot(
        x_ref[...], w_ref[...], preferred_element_type=jnp.float32
    ).astype(jnp.bfloat16)


def project_values(window, w_all, width):
    return pl.pallas_call(
        values_kernel,
        out_shape=jax.ShapeDtypeStruct((WINDOW, width), jnp.bfloat16),
        grid=(N_BLOCKS,),
        in_specs=[
            pl.BlockSpec((BLOCK, D), lambda i: (i, 0)),
            pl.BlockSpec((D, width), lambda i: (0, 2)),
        ],
        out_specs=pl.BlockSpec((BLOCK, width), lambda i: (i, 0)),
        compiler_params=pltpu.CompilerParams(vmem_limit_bytes=32 << 20),
        name="values",
    )(window, w_all)


def attend_kernel(
    lo_ref, hi_ref, q_ref, k_ref, v_ref, squares_ref, q_gain_ref, k_gain_ref, own_ref, near_ref,
    out_ref, q_hat, k_hat, s_ref,
):
    total = squares_ref[0]
    for device in range(1, N_HEAD):
        total = total + squares_ref[device]
    factors = lax.rsqrt(total / (HEADS * HEAD_DIM) + EPS)
    heads_here = q_ref.shape[1] // HEAD_DIM

    def unit(source, target, gain, block, row):
        factor = jnp.transpose(jnp.broadcast_to(factors[row : row + 1], (128, BLOCK)))
        rows = slice(block * BLOCK, block * BLOCK + BLOCK)
        for head in range(heads_here):
            cols = slice(head * HEAD_DIM, head * HEAD_DIM + HEAD_DIM)
            target[rows, cols] = (source[rows, cols] * factor * gain[:, cols]).astype(jnp.bfloat16)

    for block in range(N_BLOCKS):
        unit(k_ref, k_hat, k_gain_ref, block, block)
    for block in range(Q_BLOCKS):
        unit(q_ref, q_hat, q_gain_ref, block, N_BLOCKS + block)

    scale = 1.0 / math.sqrt(HEAD_DIM)
    for block in range(Q_BLOCKS):
        first, last = lo_ref[block], hi_ref[block]
        r0 = block * BLOCK
        own = own_ref[r0 : r0 + BLOCK, :]
        for head in range(heads_here):
            c0 = head * HEAD_DIM
            q = q_hat[r0 : r0 + BLOCK, c0 : c0 + HEAD_DIM]

            def scores(c, top):
                k = k_hat[pl.ds(c * CHUNK, CHUNK), c0 : c0 + HEAD_DIM]
                s = lax.dot_general(
                    q, k, (((1,), (1,)), ((), ())), preferred_element_type=jnp.float32
                )
                s = jnp.where(own == near_ref[c], s * scale, NEG)
                s_ref[c] = s
                for part in range(CHUNK // 128):
                    top = jnp.maximum(top, s[:, part * 128 : part * 128 + 128])
                return top

            top = lax.fori_loop(first, last, scores, jnp.full((BLOCK, 128), NEG, jnp.float32))
            highest = jnp.max(top, axis=1, keepdims=True)

            def expos(c, total):
                e = jnp.exp(s_ref[c] - highest)
                s_ref[c] = e
                for part in range(CHUNK // 128):
                    total = total + e[:, part * 128 : part * 128 + 128]
                return total

            total = lax.fori_loop(first, last, expos, jnp.zeros((BLOCK, 128), jnp.float32))
            inverse = 1.0 / jnp.sum(total, axis=1, keepdims=True)

            def mix(c, acc):
                w = (s_ref[c] * inverse).astype(jnp.bfloat16)
                v = v_ref[pl.ds(c * CHUNK, CHUNK), c0 : c0 + HEAD_DIM]
                return acc + jnp.dot(w, v, preferred_element_type=jnp.float32)

            acc = lax.fori_loop(first, last, mix, jnp.zeros((BLOCK, HEAD_DIM), jnp.float32))
            out_ref[r0 : r0 + BLOCK, c0 : c0 + HEAD_DIM] = acc.astype(jnp.bfloat16)


def attend(lo, hi, q, k, v, squares, q_gain, k_gain, own, near):
    width = q.shape[1]
    return pl.pallas_call(
        attend_kernel,
        out_shape=jax.ShapeDtypeStruct((ROWS, width), jnp.bfloat16),
        in_specs=[SMEM, SMEM] + [VMEM] * 8,
        out_specs=VMEM,
        scratch_shapes=[
            pltpu.VMEM((ROWS, width), jnp.bfloat16),
            pltpu.VMEM((WINDOW, width), jnp.bfloat16),
            pltpu.VMEM((WINDOW // CHUNK, BLOCK, CHUNK), jnp.float32),
        ],
        compiler_params=pltpu.CompilerParams(vmem_limit_bytes=32 << 20),
        name="attend",
    )(lo, hi, q, k, v, squares, q_gain, k_gain, own, near)


def on_device(tokens, ln_gain, w_query, w_key, w_value, q_gain, k_gain, seg_ids):
    width = w_query.shape[1]
    w_all = jnp.concatenate([w_query, w_key, w_value], axis=1)
    w_all = copies_to_all(w_all, "seq", NY, OVER_Y).reshape(NY * SHARD_ROWS, 3 * width)
    w_all, tokens, seg_ids = lax.optimization_barrier((w_all, tokens, seg_ids))
    w_all = lax.all_gather(w_all, "seq", axis=0, axis_index_groups=OVER_Z, tiled=True)

    normed = norm(tokens, ln_gain[None, :])

    me = lax.axis_index("head")
    near_rows = lax.dynamic_slice_in_dim(normed, me * NEAR_PART, NEAR_PART, 0)
    last_rows = lax.dynamic_slice_in_dim(normed, ROWS - FAR + me * FAR_PART, FAR_PART, 0)
    first_rows = lax.dynamic_slice_in_dim(normed, me * FAR_PART, FAR_PART, 0)
    left = jnp.concatenate([shifted(last_rows, 2), shifted(near_rows, 1)], axis=0)
    right = jnp.concatenate([shifted(near_rows, -1), shifted(first_rows, -2)], axis=0)
    own = jnp.concatenate([left, right], axis=0)
    before = along_x(own, 1)
    after = along_x(own, -1)
    across_left = along_x(before[:HALF], 1)
    across_right = along_x(after[HALF:], -1)
    pairs = [
        (own[:HALF], own[HALF:]),
        (before[:HALF], before[HALF:]),
        (after[:HALF], after[HALF:]),
        (across_left, across_right),
    ]
    twins = [other_core(t) for t in (own, before, after, across_left, across_right)]
    pairs += [(t[:HALF], t[HALF:]) for t in twins[:3]] + [(twins[3], twins[4])]
    x, core = me // 2, me % 2
    shards = jnp.stack(
        [2 * ((x + by) % NX) + c for c in (core, 1 - core) for by in (0, NX - 1, 1, 2)]
    ).astype(jnp.int32)
    window = window_of(shards, normed, [half for pair in pairs for half in pair])

    marks = seg_ids + 1
    sent = marks.astype(jnp.bfloat16)
    near = jnp.concatenate(
        [
            shifted(sent[ROWS - FAR :], 2).astype(jnp.int32),
            shifted(sent, 1).astype(jnp.int32),
            marks,
            shifted(sent, -1).astype(jnp.int32),
            shifted(sent[:FAR], -2).astype(jnp.int32),
        ]
    )
    blocks = marks.reshape(-1, BLOCK)
    low, high = blocks[:, :1], blocks[:, -1:]
    hit = (near[None, :] >= low) & (near[None, :] <= high)
    spots = jnp.arange(WINDOW, dtype=jnp.int32)[None, :]
    lo = jnp.min(jnp.where(hit, spots, WINDOW), axis=1) // CHUNK
    hi = jnp.max(jnp.where(hit, spots, -1), axis=1) // CHUNK + 1

    keys, key_squares, queries, query_squares = project_keys(window, w_all, width)
    squares = jnp.concatenate([key_squares, query_squares], axis=0)[:, 0]
    squares = copies_to_all(squares, "head", N_HEAD)
    values = project_values(window, w_all, width)
    return attend(
        lo,
        hi,
        queries,
        keys,
        values,
        squares,
        q_gain[None, :],
        k_gain[None, :],
        marks[:, None],
        near.reshape(WINDOW // CHUNK, 1, CHUNK),
    )


def solution(mesh):
    return jax.shard_map(
        on_device,
        mesh=mesh,
        in_specs=(
            P("seq", None),
            P(),
            P("seq", "head"),
            P("seq", "head"),
            P("seq", "head"),
            P("head"),
            P("head"),
            P("seq"),
        ),
        out_specs=P("seq", "head"),
        check_vma=False,
    )
```

```python
import math

import jax
import jax.numpy as jnp
from jax import lax
from jax.experimental import pallas as pl
from jax.experimental.pallas import tpu as pltpu
from jax.sharding import PartitionSpec as P

D = 3200
HEADS = 16
HEAD_DIM = 128
MOST = 1025
EPS = 1e-06
NX = 4
NY = 4
NZ = 16
N_SEQ = NY * NZ
N_HEAD = 8
ROWS = 768
FAR = 256
NEAR_PART = ROWS // N_HEAD
FAR_PART = FAR // N_HEAD
HALF = NEAR_PART + FAR_PART
WINDOW = 2 * FAR + 3 * ROWS
OWN = FAR + ROWS
BLOCK = 256
N_BLOCKS = WINDOW // BLOCK
Q_BLOCKS = ROWS // BLOCK
CHUNK = 256
NEG = -1e30
LIMIT = 24
SHARD_ROWS = D // N_SEQ

OVER_Y = [[y * NZ + z for y in range(NY)] for z in range(NZ)]
OVER_Z = [[y * NZ + z for z in range(NZ)] for y in range(NY)]
VMEM = pl.BlockSpec(memory_space=pltpu.VMEM)
SMEM = pl.BlockSpec(memory_space=pltpu.SMEM)
HBM = pl.BlockSpec(memory_space=pltpu.HBM)


def copies_to_all(value, axis, size, groups=None):
    stacked = jnp.broadcast_to(value[None], (size,) + value.shape)
    return lax.all_to_all(stacked, axis, 0, 0, axis_index_groups=groups)


def shifted(value, by):
    pairs = [(i, i + by) for i in range(N_SEQ) if 0 <= i + by < N_SEQ]
    return lax.ppermute(value, "seq", pairs)


def along_x(value, by):
    pairs = [(2 * x + c, 2 * ((x + by) % NX) + c) for x in range(NX) for c in range(2)]
    return lax.ppermute(value, "head", pairs)


def other_core(value):
    return lax.ppermute(value, "head", [(i, i ^ 1) for i in range(N_HEAD)])


def norm_kernel(x_ref, gain_ref, out_ref, plain, moved):
    x = x_ref[...].astype(jnp.float32)
    mean = jnp.sum(x * x, axis=1, keepdims=True) * (1.0 / D)
    plain[...] = x * lax.rsqrt(mean + EPS) * gain_ref[...]
    for z in range(NZ):
        for y in range(NY):
            source = (y * NZ + z) * SHARD_ROWS
            target = (z * NY + y) * SHARD_ROWS
            moved[:, target : target + SHARD_ROWS] = plain[:, source : source + SHARD_ROWS]
    out_ref[...] = moved[...].astype(jnp.bfloat16)


def norm(tokens, gain):
    rows = 128
    return pl.pallas_call(
        norm_kernel,
        out_shape=jax.ShapeDtypeStruct((ROWS, D), jnp.bfloat16),
        grid=(ROWS // rows,),
        in_specs=[
            pl.BlockSpec((rows, D), lambda i: (i, 0)),
            pl.BlockSpec((1, D), lambda i: (0, 0)),
        ],
        out_specs=pl.BlockSpec((rows, D), lambda i: (i, 0)),
        scratch_shapes=[pltpu.VMEM((rows, D), jnp.float32)] * 2,
        compiler_params=pltpu.CompilerParams(vmem_limit_bytes=10 << 20),
        cost_estimate=pl.CostEstimate(flops=1, transcendentals=0, bytes_accessed=1),
        name="norm",
    )(tokens, gain)


def row_squares(values):
    sums = jnp.sum(values * values, axis=1, keepdims=True)
    return jnp.transpose(jnp.broadcast_to(sums, (BLOCK, 128)))[:1]


def project_kernel(
    shards_ref, w_ref, own_ref, p0, p1, p2, p3l, p3r, p4, p5, p6, p7l, p7r,
    k_ref, q_ref, v_ref, squares_ref, x, w, sem,
):
    width = k_ref.shape[1]

    def columns(at, n):
        cols = pl.ds(at * width, width)
        return pltpu.make_async_copy(w_ref.at[:, cols], w.at[at], sem.at[n])

    def rows(ref, at, n):
        return pltpu.make_async_copy(ref, x.at[pl.ds(at, ref.shape[0])], sem.at[n])

    wq, wk, wv = columns(0, 0), columns(1, 1), columns(2, 2)
    own = rows(own_ref, 0, 3)
    pieces = [
        [rows(p0, ROWS, 4), rows(p1, ROWS + BLOCK, 5)],
        [rows(p2, ROWS + 2 * BLOCK, 6), rows(p3l, ROWS + 3 * BLOCK, 7)]
        + [rows(p3r, ROWS + 3 * BLOCK + HALF, 8)],
        [rows(p4, ROWS + 4 * BLOCK, 9), rows(p5, ROWS + 5 * BLOCK, 10)],
        [rows(p6, ROWS + 6 * BLOCK, 11), rows(p7l, ROWS + 7 * BLOCK, 12)]
        + [rows(p7r, ROWS + 7 * BLOCK + HALF, 13)],
    ]
    wk.start()
    own.start()
    for pair in pieces:
        for copy in pair:
            copy.start()
    wq.start()
    wv.start()

    def project(which, target, first):
        def dot(at, n):
            y = jnp.dot(x[at : at + n, :], w[which], preferred_element_type=jnp.float32)
            return y.astype(target.dtype)

        for block in range(Q_BLOCKS):
            at = block * BLOCK
            target[OWN + at : OWN + at + BLOCK, :] = dot(at, BLOCK)
        for pair in range(N_HEAD // 2):
            if first:
                for copy in pieces[pair]:
                    copy.wait()
            y = dot(ROWS + pair * 2 * BLOCK, 2 * BLOCK)
            for half in range(2):
                shard = shards_ref[2 * pair + half]
                far, near = shard * FAR_PART, shard * NEAR_PART
                part = y[half * BLOCK : half * BLOCK + BLOCK]
                places = (
                    (far, 0, FAR_PART),
                    (FAR + near, FAR_PART, NEAR_PART),
                    (OWN + ROWS + near, HALF, NEAR_PART),
                    (OWN + 2 * ROWS + far, HALF + NEAR_PART, FAR_PART),
                )
                for to, start, n in places:
                    target[pl.ds(pl.multiple_of(to, 32), n), :] = part[start : start + n]

    wk.wait()
    own.wait()
    project(1, k_ref, True)
    wq.wait()
    for block in range(Q_BLOCKS):
        here = slice(block * BLOCK, block * BLOCK + BLOCK)
        q_ref[here, :] = jnp.dot(x[here, :], w[0], preferred_element_type=jnp.float32)
    wv.wait()
    project(2, v_ref, False)
    for source, count, to in ((k_ref, N_BLOCKS, 0), (q_ref, Q_BLOCKS, N_BLOCKS)):
        for block in range(count):
            here = slice(block * BLOCK, block * BLOCK + BLOCK)
            squares_ref[to + block : to + block + 1, :] = row_squares(source[here, :])


def project(shards, w_all, own, pieces, width):
    return pl.pallas_call(
        project_kernel,
        out_shape=(
            jax.ShapeDtypeStruct((WINDOW, width), jnp.float32),
            jax.ShapeDtypeStruct((ROWS, width), jnp.float32),
            jax.ShapeDtypeStruct((WINDOW, width), jnp.bfloat16),
            jax.ShapeDtypeStruct((N_BLOCKS + Q_BLOCKS, BLOCK), jnp.float32),
        ),
        in_specs=[SMEM] + [HBM] * (2 + len(pieces)),
        out_specs=(VMEM,) * 4,
        scratch_shapes=[
            pltpu.VMEM((WINDOW, D), jnp.bfloat16),
            pltpu.VMEM((3, D, width), jnp.bfloat16),
            pltpu.SemaphoreType.DMA((14,)),
        ],
        compiler_params=pltpu.CompilerParams(vmem_limit_bytes=40 << 20),
        name="project",
    )(shards, w_all, own, *pieces)


def attend_kernel(
    lo_ref, hi_ref, q_ref, k_ref, v_ref, squares_ref, q_gain_ref, k_gain_ref, own_ref, near_ref,
    out_ref, q_hat, k_hat, s_ref,
):
    total = squares_ref[0]
    for device in range(1, N_HEAD):
        total = total + squares_ref[device]
    factors = lax.rsqrt(total / (HEADS * HEAD_DIM) + EPS)
    heads_here = q_ref.shape[1] // HEAD_DIM

    def unit(source, target, gain, block, row):
        factor = jnp.transpose(jnp.broadcast_to(factors[row : row + 1], (128, BLOCK)))
        rows = slice(block * BLOCK, block * BLOCK + BLOCK)
        for head in range(heads_here):
            cols = slice(head * HEAD_DIM, head * HEAD_DIM + HEAD_DIM)
            target[rows, cols] = (source[rows, cols] * factor * gain[:, cols]).astype(jnp.bfloat16)

    for block in range(N_BLOCKS):
        unit(k_ref, k_hat, k_gain_ref, block, block)
    for block in range(Q_BLOCKS):
        unit(q_ref, q_hat, q_gain_ref, block, N_BLOCKS + block)

    scale = 1.0 / math.sqrt(HEAD_DIM)
    heads = range(heads_here)
    cols = [slice(head * HEAD_DIM, head * HEAD_DIM + HEAD_DIM) for head in heads]
    for block in range(Q_BLOCKS):
        first, last = lo_ref[block], hi_ref[block]
        rows = slice(block * BLOCK, block * BLOCK + BLOCK)
        own = own_ref[rows, :]

        def scores(c, tops):
            allowed = own == near_ref[c]
            new = []
            for head in heads:
                s = lax.dot_general(
                    q_hat[rows, cols[head]],
                    k_hat[pl.ds(c * CHUNK, CHUNK), cols[head]],
                    (((1,), (1,)), ((), ())),
                    preferred_element_type=jnp.float32,
                )
                s = jnp.where(allowed, s * scale, NEG)
                s_ref[head, c] = s
                top = tops[head]
                for part in range(CHUNK // 128):
                    top = jnp.maximum(top, s[:, part * 128 : part * 128 + 128])
                new.append(top)
            return tuple(new)

        lowest = jnp.full((BLOCK, 128), NEG, jnp.float32)
        tops = lax.fori_loop(first, last, scores, (lowest,) * heads_here)
        highest = [jnp.max(top, axis=1, keepdims=True) for top in tops]

        def expos(c, totals):
            new = []
            for head in heads:
                e = jnp.exp(s_ref[head, c] - highest[head])
                s_ref[head, c] = e
                total = totals[head]
                for part in range(CHUNK // 128):
                    total = total + e[:, part * 128 : part * 128 + 128]
                new.append(total)
            return tuple(new)

        zeros = jnp.zeros((BLOCK, 128), jnp.float32)
        totals = lax.fori_loop(first, last, expos, (zeros,) * heads_here)
        inverse = [1.0 / jnp.sum(total, axis=1, keepdims=True) for total in totals]

        def mix(c, accs):
            new = []
            for head in heads:
                w = (s_ref[head, c] * inverse[head]).astype(jnp.bfloat16)
                v = v_ref[pl.ds(c * CHUNK, CHUNK), cols[head]]
                new.append(accs[head] + jnp.dot(w, v, preferred_element_type=jnp.float32))
            return tuple(new)

        accs = lax.fori_loop(first, last, mix, (zeros,) * heads_here)
        for head in heads:
            out_ref[rows, cols[head]] = accs[head].astype(jnp.bfloat16)


def attend(lo, hi, q, k, v, squares, q_gain, k_gain, own, near):
    width = q.shape[1]
    return pl.pallas_call(
        attend_kernel,
        out_shape=jax.ShapeDtypeStruct((ROWS, width), jnp.bfloat16),
        in_specs=[SMEM, SMEM] + [VMEM] * 8,
        out_specs=VMEM,
        scratch_shapes=[
            pltpu.VMEM((ROWS, width), jnp.bfloat16),
            pltpu.VMEM((WINDOW, width), jnp.bfloat16),
            pltpu.VMEM((width // HEAD_DIM, WINDOW // CHUNK, BLOCK, CHUNK), jnp.float32),
        ],
        compiler_params=pltpu.CompilerParams(vmem_limit_bytes=LIMIT << 20),
        name="attend",
    )(lo, hi, q, k, v, squares, q_gain, k_gain, own, near)


def on_device(tokens, ln_gain, w_query, w_key, w_value, q_gain, k_gain, seg_ids):
    width = w_query.shape[1]
    w_all = jnp.concatenate([w_query, w_key, w_value], axis=1)
    w_all = copies_to_all(w_all, "seq", NY, OVER_Y).reshape(NY * SHARD_ROWS, 3 * width)
    normed = norm(tokens, ln_gain[None, :])
    w_all, normed, seg_ids = lax.optimization_barrier((w_all, normed, seg_ids))
    w_all = lax.all_gather(w_all, "seq", axis=0, axis_index_groups=OVER_Z, tiled=True)

    me = lax.axis_index("head")
    near_rows = lax.dynamic_slice_in_dim(normed, me * NEAR_PART, NEAR_PART, 0)
    last_rows = lax.dynamic_slice_in_dim(normed, ROWS - FAR + me * FAR_PART, FAR_PART, 0)
    first_rows = lax.dynamic_slice_in_dim(normed, me * FAR_PART, FAR_PART, 0)
    left = jnp.concatenate([shifted(last_rows, 2), shifted(near_rows, 1)], axis=0)
    right = jnp.concatenate([shifted(near_rows, -1), shifted(first_rows, -2)], axis=0)
    own = jnp.concatenate([left, right], axis=0)
    before = along_x(own, 1)
    after = along_x(own, -1)
    across_left = along_x(before[:HALF], 1)
    across_right = along_x(after[HALF:], -1)
    pieces = (own, before, after, across_left, across_right)
    pieces += tuple(other_core(piece) for piece in pieces)
    x, core = me // 2, me % 2
    shards = jnp.stack(
        [2 * ((x + by) % NX) + c for c in (core, 1 - core) for by in (0, NX - 1, 1, 2)]
    ).astype(jnp.int32)

    marks = seg_ids + 1
    sent = marks.astype(jnp.bfloat16)
    near = jnp.concatenate(
        [
            shifted(sent[ROWS - FAR :], 2).astype(jnp.int32),
            shifted(sent, 1).astype(jnp.int32),
            marks,
            shifted(sent, -1).astype(jnp.int32),
            shifted(sent[:FAR], -2).astype(jnp.int32),
        ]
    )
    blocks = marks.reshape(-1, BLOCK)
    low, high = blocks[:, :1], blocks[:, -1:]
    hit = (near[None, :] >= low) & (near[None, :] <= high)
    spots = jnp.arange(WINDOW, dtype=jnp.int32)[None, :]
    lo = jnp.min(jnp.where(hit, spots, WINDOW), axis=1) // CHUNK
    hi = jnp.max(jnp.where(hit, spots, -1), axis=1) // CHUNK + 1

    w_all = pltpu.with_memory_space_constraint(w_all, pltpu.HBM)
    keys, queries, values, squares = project(shards, w_all, normed, pieces, width)
    squares = copies_to_all(squares, "head", N_HEAD)
    return attend(
        lo,
        hi,
        queries,
        keys,
        values,
        squares,
        q_gain[None, :],
        k_gain[None, :],
        marks[:, None],
        near.reshape(WINDOW // CHUNK, 1, CHUNK),
    )


def solution(mesh):
    return jax.shard_map(
        on_device,
        mesh=mesh,
        in_specs=(
            P("seq", None),
            P(),
            P("seq", "head"),
            P("seq", "head"),
            P("seq", "head"),
            P("head"),
            P("head"),
            P("seq"),
        ),
        out_specs=P("seq", "head"),
        check_vma=False,
    )
```

```python
import math

import jax
import jax.numpy as jnp
from jax import lax
from jax.experimental import pallas as pl
from jax.experimental.pallas import tpu as pltpu
from jax.sharding import PartitionSpec as P

D = 3200
HEADS = 16
HEAD_DIM = 128
MOST = 1025
EPS = 1e-06
NY = 4
NZ = 16
N_SEQ = NY * NZ
N_HEAD = 8
ROWS = 768
FAR = 256
WINDOW = 2 * FAR + 3 * ROWS
OWN = FAR + ROWS
BLOCK = 256
N_BLOCKS = WINDOW // BLOCK
Q_BLOCKS = ROWS // BLOCK
CHUNK = 256
NEG = -1e30
BEYOND = 1e6
SHARD_ROWS = D // N_SEQ
MARK_ROWS = 8

OVER_Y = [[y * NZ + z for y in range(NY)] for z in range(NZ)]
OVER_Z = [[y * NZ + z for z in range(NZ)] for y in range(NY)]
VMEM = pl.BlockSpec(memory_space=pltpu.VMEM)
SMEM = pl.BlockSpec(memory_space=pltpu.SMEM)
HBM = pl.BlockSpec(memory_space=pltpu.HBM)


def copies_to_all(value, axis, size, groups=None):
    stacked = jnp.broadcast_to(value[None], (size,) + value.shape)
    return lax.all_to_all(stacked, axis, 0, 0, axis_index_groups=groups)


def shifted(value, by):
    pairs = [(i, i + by) for i in range(N_SEQ) if 0 <= i + by < N_SEQ]
    return lax.ppermute(value, "seq", pairs)


def norm_kernel(x_ref, gain_ref, out_ref, moved_ref):
    x = x_ref[...].astype(jnp.float32)
    mean = jnp.sum(x * x, axis=1, keepdims=True) * (1.0 / D)
    out_ref[...] = (x * lax.rsqrt(mean + EPS) * gain_ref[...]).astype(jnp.bfloat16)
    for z in range(NZ):
        for y in range(NY):
            source = (y * NZ + z) * SHARD_ROWS
            target = (z * NY + y) * SHARD_ROWS
            moved_ref[:, target : target + SHARD_ROWS] = out_ref[:, source : source + SHARD_ROWS]


def norm(tokens, gain):
    rows = 128
    block = pl.BlockSpec((rows, D), lambda i: (i, 0))
    shape = jax.ShapeDtypeStruct((ROWS, D), jnp.bfloat16)
    return pl.pallas_call(
        norm_kernel,
        out_shape=(shape, shape),
        grid=(ROWS // rows,),
        in_specs=[block, pl.BlockSpec((1, D), lambda i: (0, 0))],
        out_specs=(block, block),
        compiler_params=pltpu.CompilerParams(vmem_limit_bytes=10 << 20),
        name="norm",
    )(tokens, gain)


def row_squares(values):
    sums = jnp.sum(values * values, axis=1, keepdims=True)
    return jnp.transpose(jnp.broadcast_to(sums, (BLOCK, 128)))[:1]


def keys_kernel(x_ref, w_ref, k_ref, squares_ref):
    for block in range(Q_BLOCKS):
        rows = slice(block * BLOCK, block * BLOCK + BLOCK)
        k = jnp.dot(x_ref[rows, :], w_ref[...], preferred_element_type=jnp.float32)
        k_ref[rows, :] = k
        squares_ref[block : block + 1, :] = row_squares(k)


def project_keys(x, w):
    width = w.shape[1]
    return pl.pallas_call(
        keys_kernel,
        out_shape=(
            jax.ShapeDtypeStruct((ROWS, width), jnp.float32),
            jax.ShapeDtypeStruct((Q_BLOCKS, BLOCK), jnp.float32),
        ),
        in_specs=[VMEM, VMEM],
        out_specs=(VMEM, VMEM),
        compiler_params=pltpu.CompilerParams(vmem_limit_bytes=12 << 20),
        name="keys",
    )(x, w)


def values_kernel(x_ref, w_ref, q_ref, squares_ref, v_ref, last_ref, first_ref, w, sem):
    width = v_ref.shape[1]
    loads = [
        pltpu.make_async_copy(w_ref.at[:, pl.ds(n * width, width)], w.at[n], sem.at[n])
        for n in range(2)
    ]
    loads[1].start()
    loads[0].start()
    loads[1].wait()
    for block in range(Q_BLOCKS):
        rows = slice(block * BLOCK, block * BLOCK + BLOCK)
        q = jnp.dot(x_ref[rows, :], w[1], preferred_element_type=jnp.float32)
        q_ref[rows, :] = q
        squares_ref[block : block + 1, :] = row_squares(q)
    loads[0].wait()
    for block in range(Q_BLOCKS):
        rows = slice(block * BLOCK, block * BLOCK + BLOCK)
        v_ref[rows, :] = jnp.dot(
            x_ref[rows, :], w[0], preferred_element_type=jnp.float32
        ).astype(jnp.bfloat16)
    last_ref[...] = v_ref[ROWS - FAR :, :]
    first_ref[...] = v_ref[:FAR, :]


def project_values(x, w):
    width = w.shape[1] // 2
    far = jax.ShapeDtypeStruct((FAR, width), jnp.bfloat16)
    return pl.pallas_call(
        values_kernel,
        out_shape=(
            jax.ShapeDtypeStruct((ROWS, width), jnp.float32),
            jax.ShapeDtypeStruct((Q_BLOCKS, BLOCK), jnp.float32),
            jax.ShapeDtypeStruct((ROWS, width), jnp.bfloat16),
            far,
            far,
        ),
        in_specs=[VMEM, HBM],
        out_specs=(VMEM,) * 5,
        scratch_shapes=[
            pltpu.VMEM((2, D, width), jnp.bfloat16),
            pltpu.SemaphoreType.DMA((2,)),
        ],
        compiler_params=pltpu.CompilerParams(vmem_limit_bytes=14 << 20),
        name="values",
    )(x, w)


def head_factors(squares_ref):
    total = squares_ref[0]
    for device in range(1, N_HEAD):
        total = total + squares_ref[device]
    return lax.rsqrt(total / (HEADS * HEAD_DIM) + EPS)


def unit(source, target, gain_ref, factors):
    for block in range(Q_BLOCKS):
        factor = jnp.transpose(jnp.broadcast_to(factors[block : block + 1], (128, BLOCK)))
        rows = slice(block * BLOCK, block * BLOCK + BLOCK)
        for start in range(0, source.shape[1], HEAD_DIM):
            cols = slice(start, start + HEAD_DIM)
            target[rows, cols] = (source[rows, cols] * factor * gain_ref[:, cols]).astype(
                jnp.bfloat16
            )


def unit_keys_kernel(k_ref, squares_ref, gain_ref, marks_ref, out_ref, last_ref, first_ref):
    unit(k_ref, out_ref, gain_ref, head_factors(squares_ref))
    out_ref[ROWS:, :] = marks_ref[...]
    last_ref[:FAR, :] = out_ref[ROWS - FAR : ROWS, :]
    first_ref[:FAR, :] = out_ref[:FAR, :]
    spare = jnp.zeros((MARK_ROWS - 1, out_ref.shape[1]), jnp.float32)
    marks = marks_ref[...].astype(jnp.float32)
    last_ref[FAR:, :] = jnp.concatenate([marks[Q_BLOCKS - 1 : Q_BLOCKS], spare]).astype(jnp.bfloat16)
    first_ref[FAR:, :] = jnp.concatenate([marks[:1], spare]).astype(jnp.bfloat16)


def unit_keys(k, squares, gain, marks):
    width = k.shape[1]
    far = jax.ShapeDtypeStruct((FAR + MARK_ROWS, width), jnp.bfloat16)
    return pl.pallas_call(
        unit_keys_kernel,
        out_shape=(jax.ShapeDtypeStruct((ROWS + MARK_ROWS, width), jnp.bfloat16), far, far),
        in_specs=[VMEM] * 4,
        out_specs=(VMEM,) * 3,
        compiler_params=pltpu.CompilerParams(vmem_limit_bytes=8 << 20),
        name="unit_keys",
    )(k, squares, gain, marks)


def attend_kernel(
    q_ref, squares_ref, q_gain_ref, own_ref, ka, kb, kc, kd, ke, va, vb, vc, vd, ve,
    out_ref, q_hat, k_win, v_win, near_ref, s_ref,
):
    start = 0
    for k_part, v_part in ((ka, va), (kb, vb), (kc, vc), (kd, vd), (ke, ve)):
        rows = v_part.shape[0]
        k_win[start : start + rows, :] = k_part[:rows, :]
        v_win[start : start + rows, :] = v_part[...]
        marks = k_part[rows:, :].astype(jnp.float32)
        if start > OWN:
            marks = jnp.where(marks == 0, BEYOND, marks)
        for n in range(rows // CHUNK):
            near_ref[start // CHUNK + n] = marks[n : n + 1]
        start += rows
    unit(q_ref, q_hat, q_gain_ref, head_factors(squares_ref))

    scale = 1.0 / math.sqrt(HEAD_DIM)
    heads = range(q_ref.shape[1] // HEAD_DIM)
    cols = [slice(head * HEAD_DIM, head * HEAD_DIM + HEAD_DIM) for head in heads]
    for block in range(Q_BLOCKS):
        rows = slice(block * BLOCK, block * BLOCK + BLOCK)
        own = own_ref[rows, :]
        low, high = jnp.min(own), jnp.max(own)
        near = near_ref[...]
        below = jnp.sum((near < low).astype(jnp.float32)).astype(jnp.int32)
        within = jnp.sum((near <= high).astype(jnp.float32)).astype(jnp.int32)
        first, last = below // CHUNK, (within + CHUNK - 1) // CHUNK

        def scores(c, tops):
            allowed = own == near_ref[c]
            new = []
            for head in heads:
                s = lax.dot_general(
                    q_hat[rows, cols[head]],
                    k_win[pl.ds(c * CHUNK, CHUNK), cols[head]],
                    (((1,), (1,)), ((), ())),
                    preferred_element_type=jnp.float32,
                )
                s = jnp.where(allowed, s * scale, NEG)
                s_ref[head, c] = s
                top = tops[head]
                for part in range(CHUNK // 128):
                    top = jnp.maximum(top, s[:, part * 128 : part * 128 + 128])
                new.append(top)
            return tuple(new)

        lowest = jnp.full((BLOCK, 128), NEG, jnp.float32)
        tops = lax.fori_loop(first, last, scores, (lowest,) * len(heads))
        highest = [jnp.max(top, axis=1, keepdims=True) for top in tops]

        def expos(c, totals):
            new = []
            for head in heads:
                e = jnp.exp(s_ref[head, c] - highest[head])
                s_ref[head, c] = e
                total = totals[head]
                for part in range(CHUNK // 128):
                    total = total + e[:, part * 128 : part * 128 + 128]
                new.append(total)
            return tuple(new)

        zeros = jnp.zeros((BLOCK, 128), jnp.float32)
        totals = lax.fori_loop(first, last, expos, (zeros,) * len(heads))
        inverse = [1.0 / jnp.sum(total, axis=1, keepdims=True) for total in totals]

        def mix(c, accs):
            new = []
            for head in heads:
                w = (s_ref[head, c] * inverse[head]).astype(jnp.bfloat16)
                v = v_win[pl.ds(c * CHUNK, CHUNK), cols[head]]
                new.append(accs[head] + jnp.dot(w, v, preferred_element_type=jnp.float32))
            return tuple(new)

        accs = lax.fori_loop(first, last, mix, (zeros,) * len(heads))
        for head in heads:
            out_ref[rows, cols[head]] = accs[head].astype(jnp.bfloat16)


def attend(q, squares, gain, own, k_parts, v_parts):
    width = q.shape[1]
    return pl.pallas_call(
        attend_kernel,
        out_shape=jax.ShapeDtypeStruct((ROWS, width), jnp.bfloat16),
        in_specs=[VMEM] * 14,
        out_specs=VMEM,
        scratch_shapes=[
            pltpu.VMEM((ROWS, width), jnp.bfloat16),
            pltpu.VMEM((WINDOW, width), jnp.bfloat16),
            pltpu.VMEM((WINDOW, width), jnp.bfloat16),
            pltpu.VMEM((WINDOW // CHUNK, 1, CHUNK), jnp.float32),
            pltpu.VMEM((width // HEAD_DIM, WINDOW // CHUNK, BLOCK, CHUNK), jnp.float32),
        ],
        compiler_params=pltpu.CompilerParams(vmem_limit_bytes=24 << 20),
        name="attend",
    )(q, squares, gain, own, *k_parts, *v_parts)


def on_device(tokens, ln_gain, w_query, w_key, w_value, q_gain, k_gain, seg_ids):
    width = w_query.shape[1]
    vq = jnp.concatenate([w_value, w_query], axis=1)
    vq = copies_to_all(vq, "seq", NY, OVER_Y).reshape(NY * SHARD_ROWS, 2 * width)
    vq, w_key = lax.optimization_barrier((vq, w_key))
    vq = lax.all_gather(vq, "seq", axis=0, axis_index_groups=OVER_Z, tiled=True)
    k_z = lax.all_gather(w_key, "seq", axis=0, axis_index_groups=OVER_Z)
    k_z, tokens, seg_ids = lax.optimization_barrier((k_z, tokens, seg_ids))
    k_all = copies_to_all(k_z.reshape(NZ * SHARD_ROWS, width), "seq", NY, OVER_Y)
    normed, moved = norm(tokens, ln_gain[None, :])
    marks = (seg_ids + 1).astype(jnp.float32)
    mark_rows = jnp.pad(marks.reshape(-1, width), ((0, MARK_ROWS - ROWS // width), (0, 0)))

    keys, squares = project_keys(normed, k_all.reshape(D, width))
    squares = copies_to_all(squares, "head", N_HEAD)
    k_own, k_last, k_first = unit_keys(
        keys, squares, k_gain[None, :], mark_rows.astype(jnp.bfloat16)
    )
    k_parts = (shifted(k_last, 2), shifted(k_own, 1), k_own, shifted(k_own, -1), shifted(k_first, -2))

    vq = pltpu.with_memory_space_constraint(vq, pltpu.HBM)
    queries, squares, v_own, v_last, v_first = project_values(moved, vq)
    squares = copies_to_all(squares, "head", N_HEAD)
    v_parts = (shifted(v_last, 2), shifted(v_own, 1), v_own, shifted(v_own, -1), shifted(v_first, -2))
    return attend(queries, squares, q_gain[None, :], marks[:, None], k_parts, v_parts)


def solution(mesh):
    return jax.shard_map(
        on_device,
        mesh=mesh,
        in_specs=(
            P("seq", None),
            P(),
            P("seq", "head"),
            P("seq", "head"),
            P("seq", "head"),
            P("head"),
            P("head"),
            P("seq"),
        ),
        out_specs=P("seq", "head"),
        check_vma=False,
    )
```

```python
import math

import jax
import jax.numpy as jnp
from jax import lax
from jax.experimental import pallas as pl
from jax.experimental.pallas import tpu as pltpu
from jax.sharding import PartitionSpec as P

D = 3200
HEADS = 16
HEAD_DIM = 128
MOST = 1025
EPS = 1e-06
NY = 4
NZ = 16
N_SEQ = NY * NZ
N_HEAD = 8
ROWS = 768
FAR = 256
WINDOW = 2 * FAR + 3 * ROWS
OWN = FAR + ROWS
BLOCK = 256
N_BLOCKS = WINDOW // BLOCK
Q_BLOCKS = ROWS // BLOCK
CHUNK = 256
NEG = -1e30
BEYOND = 1e6
SHARD_ROWS = D // N_SEQ
MARK_ROWS = 8

OVER_Y = [[y * NZ + z for y in range(NY)] for z in range(NZ)]
OVER_Z = [[y * NZ + z for z in range(NZ)] for y in range(NY)]
VMEM = pl.BlockSpec(memory_space=pltpu.VMEM)
SMEM = pl.BlockSpec(memory_space=pltpu.SMEM)
HBM = pl.BlockSpec(memory_space=pltpu.HBM)


def copies_to_all(value, axis, size, groups=None):
    stacked = jnp.broadcast_to(value[None], (size,) + value.shape)
    return lax.all_to_all(stacked, axis, 0, 0, axis_index_groups=groups)


def shifted(value, by):
    pairs = [(i, i + by) for i in range(N_SEQ) if 0 <= i + by < N_SEQ]
    return lax.ppermute(value, "seq", pairs)


def normalised(x_ref, gain_ref):
    x = x_ref[...].astype(jnp.float32)
    mean = jnp.sum(x * x, axis=1, keepdims=True) * (1.0 / D)
    return (x * lax.rsqrt(mean + EPS) * gain_ref[...]).astype(jnp.bfloat16)


def norm_kernel(x_ref, gain_ref, out_ref, plain):
    plain[...] = normalised(x_ref, gain_ref)
    for z in range(NZ):
        for y in range(NY):
            source = (y * NZ + z) * SHARD_ROWS
            target = (z * NY + y) * SHARD_ROWS
            out_ref[:, target : target + SHARD_ROWS] = plain[:, source : source + SHARD_ROWS]


def norm(tokens, gain):
    rows = 128
    block = pl.BlockSpec((rows, D), lambda i: (i, 0))
    return pl.pallas_call(
        norm_kernel,
        out_shape=jax.ShapeDtypeStruct((ROWS, D), jnp.bfloat16),
        grid=(ROWS // rows,),
        in_specs=[block, pl.BlockSpec((1, D), lambda i: (0, 0))],
        out_specs=block,
        scratch_shapes=[pltpu.VMEM((rows, D), jnp.bfloat16)],
        compiler_params=pltpu.CompilerParams(vmem_limit_bytes=10 << 20),
        name="norm",
    )(tokens, gain)


def row_squares(values):
    sums = jnp.sum(values * values, axis=1, keepdims=True)
    return jnp.transpose(jnp.broadcast_to(sums, (BLOCK, 128)))[:1]


def loads_of(x_ref, x, sem):
    loads = []
    for block in range(Q_BLOCKS):
        rows = pl.ds(block * BLOCK, BLOCK)
        loads.append(pltpu.make_async_copy(x_ref.at[rows], x.at[rows], sem.at[block]))
    return loads


def values_kernel(
    x_ref, w_ref, v_ref, last_ref, first_ref, q_ref, squares_ref, x, wv, wq, sem
):
    width = wv.shape[1]
    load_v = pltpu.make_async_copy(w_ref.at[:, pl.ds(0, width)], wv, sem.at[Q_BLOCKS])
    load_q = pltpu.make_async_copy(w_ref.at[:, pl.ds(width, width)], wq, sem.at[Q_BLOCKS + 1])
    loads = loads_of(x_ref, x, sem)
    for load in (load_v, *loads, load_q):
        load.start()
    load_v.wait()
    for block in range(Q_BLOCKS):
        loads[block].wait()
        rows = slice(block * BLOCK, block * BLOCK + BLOCK)
        v = jnp.dot(x[rows, :], wv[...], preferred_element_type=jnp.float32).astype(jnp.bfloat16)
        v_ref[rows, :] = v
        if block == 0:
            first_ref[...] = v
        if block == Q_BLOCKS - 1:
            last_ref[...] = v
    load_q.wait()
    for block in range(Q_BLOCKS):
        rows = slice(block * BLOCK, block * BLOCK + BLOCK)
        q = jnp.dot(x[rows, :], wq[...], preferred_element_type=jnp.float32)
        q_ref[rows, :] = q
        squares_ref[block : block + 1, :] = row_squares(q)


def project_values(x, w, width):
    far = jax.ShapeDtypeStruct((FAR, width), jnp.bfloat16)
    return pl.pallas_call(
        values_kernel,
        out_shape=(
            jax.ShapeDtypeStruct((ROWS, width), jnp.bfloat16),
            far,
            far,
            jax.ShapeDtypeStruct((ROWS, width), jnp.float32),
            jax.ShapeDtypeStruct((Q_BLOCKS, BLOCK), jnp.float32),
        ),
        in_specs=[HBM, HBM],
        out_specs=(VMEM,) * 5,
        scratch_shapes=[
            pltpu.VMEM((ROWS, D), jnp.bfloat16),
            pltpu.VMEM((D, width), jnp.bfloat16),
            pltpu.VMEM((D, width), jnp.bfloat16),
            pltpu.SemaphoreType.DMA((Q_BLOCKS + 2,)),
        ],
        compiler_params=pltpu.CompilerParams(vmem_limit_bytes=16 << 20),
        name="values",
    )(x, w)


def keys_kernel(x_ref, gain_ref, w_ref, k_ref, squares_ref, x, w, sem):
    load_w = pltpu.make_async_copy(w_ref, w, sem.at[Q_BLOCKS])
    loads = loads_of(x_ref, x, sem)
    for load in (loads[0], load_w, *loads[1:]):
        load.start()
    for block in range(Q_BLOCKS):
        rows = slice(block * BLOCK, block * BLOCK + BLOCK)
        loads[block].wait()
        normed = normalised(x.at[rows, :], gain_ref)
        if block == 0:
            load_w.wait()
        k = jnp.dot(normed, w[...], preferred_element_type=jnp.float32)
        k_ref[rows, :] = k
        squares_ref[block : block + 1, :] = row_squares(k)


def project_keys(tokens, gain, w):
    width = w.shape[1]
    return pl.pallas_call(
        keys_kernel,
        out_shape=(
            jax.ShapeDtypeStruct((ROWS, width), jnp.float32),
            jax.ShapeDtypeStruct((Q_BLOCKS, BLOCK), jnp.float32),
        ),
        in_specs=[HBM, VMEM, HBM],
        out_specs=(VMEM,) * 2,
        scratch_shapes=[
            pltpu.VMEM((ROWS, D), jnp.bfloat16),
            pltpu.VMEM((D, width), jnp.bfloat16),
            pltpu.SemaphoreType.DMA((Q_BLOCKS + 1,)),
        ],
        compiler_params=pltpu.CompilerParams(vmem_limit_bytes=20 << 20),
        name="keys",
    )(tokens, gain, w)


def in_hbm(value):
    return pltpu.with_memory_space_constraint(value, pltpu.HBM)


def head_factors(squares_ref):
    total = squares_ref[0]
    for device in range(1, N_HEAD):
        total = total + squares_ref[device]
    return lax.rsqrt(total / (HEADS * HEAD_DIM) + EPS)


def unit(source, target, gain_ref, factors):
    for block in range(Q_BLOCKS):
        factor = jnp.transpose(jnp.broadcast_to(factors[block : block + 1], (128, BLOCK)))
        rows = slice(block * BLOCK, block * BLOCK + BLOCK)
        for start in range(0, source.shape[1], HEAD_DIM):
            cols = slice(start, start + HEAD_DIM)
            target[rows, cols] = (source[rows, cols] * factor * gain_ref[:, cols]).astype(
                jnp.bfloat16
            )


def unit_keys_kernel(k_ref, squares_ref, gain_ref, marks_ref, out_ref, last_ref, first_ref):
    unit(k_ref, out_ref, gain_ref, head_factors(squares_ref))
    out_ref[ROWS:, :] = marks_ref[...]
    last_ref[:FAR, :] = out_ref[ROWS - FAR : ROWS, :]
    first_ref[:FAR, :] = out_ref[:FAR, :]
    spare = jnp.zeros((MARK_ROWS - 1, out_ref.shape[1]), jnp.float32)
    marks = marks_ref[...].astype(jnp.float32)
    last_ref[FAR:, :] = jnp.concatenate([marks[Q_BLOCKS - 1 : Q_BLOCKS], spare]).astype(jnp.bfloat16)
    first_ref[FAR:, :] = jnp.concatenate([marks[:1], spare]).astype(jnp.bfloat16)


def unit_keys(k, squares, gain, marks):
    width = k.shape[1]
    far = jax.ShapeDtypeStruct((FAR + MARK_ROWS, width), jnp.bfloat16)
    return pl.pallas_call(
        unit_keys_kernel,
        out_shape=(jax.ShapeDtypeStruct((ROWS + MARK_ROWS, width), jnp.bfloat16), far, far),
        in_specs=[VMEM] * 4,
        out_specs=(VMEM,) * 3,
        compiler_params=pltpu.CompilerParams(vmem_limit_bytes=8 << 20),
        name="unit_keys",
    )(k, squares, gain, marks)


def attend_kernel(
    q_ref, squares_ref, q_gain_ref, own_ref, kb, kc, kd, far_a, far_e, vb, vc, vd,
    out_ref, q_hat, k_win, v_win, near_ref, s_ref,
):
    start = 0
    for k_part, v_part in ((far_a, None), (kb, vb), (kc, vc), (kd, vd), (far_e, None)):
        rows = FAR if v_part is None else ROWS
        k_win[start : start + rows, :] = k_part[:rows, :]
        if v_part is None:
            v_win[start : start + rows, :] = k_part[rows + MARK_ROWS :, :]
        else:
            v_win[start : start + rows, :] = v_part[...]
        marks = k_part[rows : rows + MARK_ROWS, :].astype(jnp.float32)
        if start > OWN:
            marks = jnp.where(marks == 0, BEYOND, marks)
        for n in range(rows // CHUNK):
            near_ref[start // CHUNK + n] = marks[n : n + 1]
        start += rows
    unit(q_ref, q_hat, q_gain_ref, head_factors(squares_ref))

    scale = 1.0 / math.sqrt(HEAD_DIM)
    heads = range(q_ref.shape[1] // HEAD_DIM)
    cols = [slice(head * HEAD_DIM, head * HEAD_DIM + HEAD_DIM) for head in heads]
    for block in range(Q_BLOCKS):
        rows = slice(block * BLOCK, block * BLOCK + BLOCK)
        own = own_ref[rows, :]
        low, high = jnp.min(own), jnp.max(own)
        near = near_ref[...]
        below = jnp.sum((near < low).astype(jnp.float32)).astype(jnp.int32)
        within = jnp.sum((near <= high).astype(jnp.float32)).astype(jnp.int32)
        first, last = below // CHUNK, (within + CHUNK - 1) // CHUNK

        def scores(c, tops):
            allowed = own == near_ref[c]
            new = []
            for head in heads:
                s = lax.dot_general(
                    q_hat[rows, cols[head]],
                    k_win[pl.ds(c * CHUNK, CHUNK), cols[head]],
                    (((1,), (1,)), ((), ())),
                    preferred_element_type=jnp.float32,
                )
                s = jnp.where(allowed, s * scale, NEG)
                s_ref[head, c] = s
                top = tops[head]
                for part in range(CHUNK // 128):
                    top = jnp.maximum(top, s[:, part * 128 : part * 128 + 128])
                new.append(top)
            return tuple(new)

        lowest = jnp.full((BLOCK, 128), NEG, jnp.float32)
        tops = lax.fori_loop(first, last, scores, (lowest,) * len(heads))
        highest = [jnp.max(top, axis=1, keepdims=True) for top in tops]

        def expos(c, totals):
            new = []
            for head in heads:
                e = jnp.exp(s_ref[head, c] - highest[head])
                s_ref[head, c] = e
                total = totals[head]
                for part in range(CHUNK // 128):
                    total = total + e[:, part * 128 : part * 128 + 128]
                new.append(total)
            return tuple(new)

        zeros = jnp.zeros((BLOCK, 128), jnp.float32)
        totals = lax.fori_loop(first, last, expos, (zeros,) * len(heads))
        inverse = [1.0 / jnp.sum(total, axis=1, keepdims=True) for total in totals]

        def mix(c, accs):
            new = []
            for head in heads:
                w = (s_ref[head, c] * inverse[head]).astype(jnp.bfloat16)
                v = v_win[pl.ds(c * CHUNK, CHUNK), cols[head]]
                new.append(accs[head] + jnp.dot(w, v, preferred_element_type=jnp.float32))
            return tuple(new)

        accs = lax.fori_loop(first, last, mix, (zeros,) * len(heads))
        for head in heads:
            out_ref[rows, cols[head]] = accs[head].astype(jnp.bfloat16)


def attend(q, squares, gain, own, k_parts, far_parts, v_parts):
    width = q.shape[1]
    return pl.pallas_call(
        attend_kernel,
        out_shape=jax.ShapeDtypeStruct((ROWS, width), jnp.bfloat16),
        in_specs=[VMEM] * 12,
        out_specs=VMEM,
        scratch_shapes=[
            pltpu.VMEM((ROWS, width), jnp.bfloat16),
            pltpu.VMEM((WINDOW, width), jnp.bfloat16),
            pltpu.VMEM((WINDOW, width), jnp.bfloat16),
            pltpu.VMEM((WINDOW // CHUNK, 1, CHUNK), jnp.float32),
            pltpu.VMEM((width // HEAD_DIM, WINDOW // CHUNK, BLOCK, CHUNK), jnp.float32),
        ],
        compiler_params=pltpu.CompilerParams(vmem_limit_bytes=24 << 20),
        name="attend",
    )(q, squares, gain, own, *k_parts, *far_parts, *v_parts)


def on_device(tokens, ln_gain, w_query, w_key, w_value, q_gain, k_gain, seg_ids):
    width = w_query.shape[1]
    vq = jnp.concatenate([w_value, w_query], axis=1)
    vq = copies_to_all(vq, "seq", NY, OVER_Y).reshape(NY * SHARD_ROWS, 2 * width)
    vq, w_key = lax.optimization_barrier((vq, w_key))
    vq = lax.all_gather(vq, "seq", axis=0, axis_index_groups=OVER_Z, tiled=True)
    k_z = lax.all_gather(w_key, "seq", axis=0, axis_index_groups=OVER_Z)
    gain = ln_gain[None, :]
    k_z, late_tokens, seg_ids = lax.optimization_barrier((k_z, tokens, seg_ids))
    k_all = copies_to_all(k_z.reshape(NZ * SHARD_ROWS, width), "seq", NY, OVER_Y)
    k_all, moved = lax.optimization_barrier((k_all, norm(late_tokens, gain)))
    moved = in_hbm(moved)
    marks = (seg_ids + 1).astype(jnp.float32)
    mark_rows = jnp.pad(marks.reshape(-1, width), ((0, MARK_ROWS - ROWS // width), (0, 0)))

    keys, squares = project_keys(in_hbm(tokens), gain, in_hbm(k_all.reshape(D, width)))
    squares = copies_to_all(squares, "head", N_HEAD)
    k_own, k_last, k_first = unit_keys(
        keys, squares, k_gain[None, :], mark_rows.astype(jnp.bfloat16)
    )
    k_parts = (shifted(k_own, 1), k_own, shifted(k_own, -1))

    vq = in_hbm(vq)
    v_own, v_last, v_first, queries, squares = project_values(moved, vq, width)
    squares = copies_to_all(squares, "head", N_HEAD)
    far_parts = (
        shifted(jnp.concatenate([k_last, v_last], axis=0), 2),
        shifted(jnp.concatenate([k_first, v_first], axis=0), -2),
    )
    v_parts = (shifted(v_own, 1), v_own, shifted(v_own, -1))
    return attend(
        queries, squares, q_gain[None, :], marks[:, None], k_parts, far_parts, v_parts
    )


def solution(mesh):
    return jax.shard_map(
        on_device,
        mesh=mesh,
        in_specs=(
            P("seq", None),
            P(),
            P("seq", "head"),
            P("seq", "head"),
            P("seq", "head"),
            P("head"),
            P("head"),
            P("seq"),
        ),
        out_specs=P("seq", "head"),
        check_vma=False,
    )
```

```python
import math

import jax
import jax.numpy as jnp
from jax import lax
from jax.experimental import pallas as pl
from jax.experimental.pallas import tpu as pltpu
from jax.sharding import PartitionSpec as P

D = 3200
HEADS = 16
HEAD_DIM = 128
MOST = 1025
EPS = 1e-06
NY = 4
NZ = 16
N_SEQ = NY * NZ
N_HEAD = 8
ROWS = 768
FAR = 256
WINDOW = 2 * FAR + 3 * ROWS
OWN = FAR + ROWS
BLOCK = 256
N_BLOCKS = WINDOW // BLOCK
Q_BLOCKS = ROWS // BLOCK
CHUNK = 256
TOGETHER = 2
PADDED = WINDOW + (TOGETHER - 1) * CHUNK
NEG = -1e30
BEYOND = 1e6
SHARD_ROWS = D // N_SEQ
MARK_ROWS = 8

OVER_Y = [[y * NZ + z for y in range(NY)] for z in range(NZ)]
OVER_Z = [[y * NZ + z for z in range(NZ)] for y in range(NY)]
VMEM = pl.BlockSpec(memory_space=pltpu.VMEM)
SMEM = pl.BlockSpec(memory_space=pltpu.SMEM)
HBM = pl.BlockSpec(memory_space=pltpu.HBM)


def copies_to_all(value, axis, size, groups=None):
    stacked = jnp.broadcast_to(value[None], (size,) + value.shape)
    return lax.all_to_all(stacked, axis, 0, 0, axis_index_groups=groups)


def shifted(value, by):
    pairs = [(i, i + by) for i in range(N_SEQ) if 0 <= i + by < N_SEQ]
    return lax.ppermute(value, "seq", pairs)


def normalised(x_ref, gain_ref):
    x = x_ref[...].astype(jnp.float32)
    mean = jnp.sum(x * x, axis=1, keepdims=True) * (1.0 / D)
    return (x * lax.rsqrt(mean + EPS) * gain_ref[...]).astype(jnp.bfloat16)


def norm_kernel(x_ref, gain_ref, out_ref, plain):
    plain[...] = normalised(x_ref, gain_ref)
    for z in range(NZ):
        for y in range(NY):
            source = (y * NZ + z) * SHARD_ROWS
            target = (z * NY + y) * SHARD_ROWS
            out_ref[:, target : target + SHARD_ROWS] = plain[:, source : source + SHARD_ROWS]


def norm(tokens, gain):
    rows = 128
    block = pl.BlockSpec((rows, D), lambda i: (i, 0))
    return pl.pallas_call(
        norm_kernel,
        out_shape=jax.ShapeDtypeStruct((ROWS, D), jnp.bfloat16),
        grid=(ROWS // rows,),
        in_specs=[block, pl.BlockSpec((1, D), lambda i: (0, 0))],
        out_specs=block,
        scratch_shapes=[pltpu.VMEM((rows, D), jnp.bfloat16)],
        compiler_params=pltpu.CompilerParams(vmem_limit_bytes=10 << 20),
        name="norm",
    )(tokens, gain)


def row_squares(values):
    sums = jnp.sum(values * values, axis=1, keepdims=True)
    return jnp.transpose(jnp.broadcast_to(sums, (BLOCK, 128)))[:1]


def loads_of(x_ref, x, sem):
    loads = []
    for block in range(Q_BLOCKS):
        rows = pl.ds(block * BLOCK, BLOCK)
        loads.append(pltpu.make_async_copy(x_ref.at[rows], x.at[rows], sem.at[block]))
    return loads


def loaded_blocks(x_ref, w_ref, at, x, w, sem):
    load_w = pltpu.make_async_copy(w_ref.at[:, pl.ds(at, w.shape[1])], w, sem.at[Q_BLOCKS])
    loads = loads_of(x_ref, x, sem)
    for load in (load_w, *loads):
        load.start()
    load_w.wait()
    for block in range(Q_BLOCKS):
        loads[block].wait()
        rows = slice(block * BLOCK, block * BLOCK + BLOCK)
        yield block, rows, jnp.dot(x[rows, :], w[...], preferred_element_type=jnp.float32)


def values_kernel(
    x_ref, w_ref, k_last, k_first, v_ref, last_ref, first_ref, x, w, sem
):
    last_ref[: FAR + MARK_ROWS, :] = k_last[...]
    first_ref[: FAR + MARK_ROWS, :] = k_first[...]
    for block, rows, y in loaded_blocks(x_ref, w_ref, 0, x, w, sem):
        v = y.astype(jnp.bfloat16)
        v_ref[rows, :] = v
        if block == 0:
            first_ref[FAR + MARK_ROWS :, :] = v
        if block == Q_BLOCKS - 1:
            last_ref[FAR + MARK_ROWS :, :] = v


def queries_kernel(x_ref, w_ref, q_ref, squares_ref, x, w, sem):
    for block, rows, q in loaded_blocks(x_ref, w_ref, w.shape[1], x, w, sem):
        q_ref[rows, :] = q
        squares_ref[block : block + 1, :] = row_squares(q)


def project(kernel, name, outs, width, x, w, *more):
    return pl.pallas_call(
        kernel,
        out_shape=outs,
        in_specs=[HBM, HBM] + [VMEM] * len(more),
        out_specs=(VMEM,) * len(outs),
        scratch_shapes=[
            pltpu.VMEM((ROWS, D), jnp.bfloat16),
            pltpu.VMEM((D, width), jnp.bfloat16),
            pltpu.SemaphoreType.DMA((Q_BLOCKS + 1,)),
        ],
        compiler_params=pltpu.CompilerParams(vmem_limit_bytes=16 << 20),
        name=name,
    )(x, w, *more)


def keys_kernel(x_ref, gain_ref, w_ref, k_ref, squares_ref, x, w, sem):
    load_w = pltpu.make_async_copy(w_ref, w, sem.at[Q_BLOCKS])
    loads = loads_of(x_ref, x, sem)
    for load in (loads[0], load_w, *loads[1:]):
        load.start()
    for block in range(Q_BLOCKS):
        rows = slice(block * BLOCK, block * BLOCK + BLOCK)
        loads[block].wait()
        normed = normalised(x.at[rows, :], gain_ref)
        if block == 0:
            load_w.wait()
        k = jnp.dot(normed, w[...], preferred_element_type=jnp.float32)
        k_ref[rows, :] = k
        squares_ref[block : block + 1, :] = row_squares(k)


def project_keys(tokens, gain, w):
    width = w.shape[1]
    return pl.pallas_call(
        keys_kernel,
        out_shape=(
            jax.ShapeDtypeStruct((ROWS, width), jnp.float32),
            jax.ShapeDtypeStruct((Q_BLOCKS, BLOCK), jnp.float32),
        ),
        in_specs=[HBM, VMEM, HBM],
        out_specs=(VMEM,) * 2,
        scratch_shapes=[
            pltpu.VMEM((ROWS, D), jnp.bfloat16),
            pltpu.VMEM((D, width), jnp.bfloat16),
            pltpu.SemaphoreType.DMA((Q_BLOCKS + 1,)),
        ],
        compiler_params=pltpu.CompilerParams(vmem_limit_bytes=20 << 20),
        name="keys",
    )(tokens, gain, w)


def in_hbm(value):
    return pltpu.with_memory_space_constraint(value, pltpu.HBM)


def head_factors(squares_ref):
    total = squares_ref[0]
    for device in range(1, N_HEAD):
        total = total + squares_ref[device]
    return lax.rsqrt(total / (HEADS * HEAD_DIM) + EPS)


def unit(source, target, gain_ref, factors):
    for block in range(Q_BLOCKS):
        factor = jnp.transpose(jnp.broadcast_to(factors[block : block + 1], (128, BLOCK)))
        rows = slice(block * BLOCK, block * BLOCK + BLOCK)
        for start in range(0, source.shape[1], HEAD_DIM):
            cols = slice(start, start + HEAD_DIM)
            target[rows, cols] = (source[rows, cols] * factor * gain_ref[:, cols]).astype(
                jnp.bfloat16
            )


def unit_keys_kernel(k_ref, squares_ref, gain_ref, marks_ref, out_ref, last_ref, first_ref):
    unit(k_ref, out_ref, gain_ref, head_factors(squares_ref))
    out_ref[ROWS:, :] = marks_ref[...]
    last_ref[:FAR, :] = out_ref[ROWS - FAR : ROWS, :]
    first_ref[:FAR, :] = out_ref[:FAR, :]
    spare = jnp.zeros((MARK_ROWS - 1, out_ref.shape[1]), jnp.float32)
    marks = marks_ref[...].astype(jnp.float32)
    last_ref[FAR:, :] = jnp.concatenate([marks[Q_BLOCKS - 1 : Q_BLOCKS], spare]).astype(jnp.bfloat16)
    first_ref[FAR:, :] = jnp.concatenate([marks[:1], spare]).astype(jnp.bfloat16)


def unit_keys(k, squares, gain, marks):
    width = k.shape[1]
    far = jax.ShapeDtypeStruct((FAR + MARK_ROWS, width), jnp.bfloat16)
    return pl.pallas_call(
        unit_keys_kernel,
        out_shape=(jax.ShapeDtypeStruct((ROWS + MARK_ROWS, width), jnp.bfloat16), far, far),
        in_specs=[VMEM] * 4,
        out_specs=(VMEM,) * 3,
        compiler_params=pltpu.CompilerParams(vmem_limit_bytes=8 << 20),
        name="unit_keys",
    )(k, squares, gain, marks)


def attend_kernel(
    marks_ref, q_ref, squares_ref, q_gain_ref, own_ref, kb, kc, kd, far_a, far_e, vb, vc, vd,
    out_ref, q_hat, k_win, v_win, near_ref, s_ref,
):
    start = 0
    for k_part, v_part in ((far_a, None), (kb, vb), (kc, vc), (kd, vd), (far_e, None)):
        rows = FAR if v_part is None else ROWS
        k_win[start : start + rows, :] = k_part[:rows, :]
        if v_part is None:
            v_win[start : start + rows, :] = k_part[rows + MARK_ROWS :, :]
        else:
            v_win[start : start + rows, :] = v_part[...]
        marks = k_part[rows : rows + MARK_ROWS, :].astype(jnp.float32)
        if start > OWN:
            marks = jnp.where(marks == 0, BEYOND, marks)
        for n in range(rows // CHUNK):
            near_ref[start // CHUNK + n] = marks[n : n + 1]
        start += rows
    k_win[WINDOW:, :] = jnp.zeros((PADDED - WINDOW, k_win.shape[1]), jnp.bfloat16)
    v_win[WINDOW:, :] = jnp.zeros((PADDED - WINDOW, v_win.shape[1]), jnp.bfloat16)
    for c in range(WINDOW // CHUNK, PADDED // CHUNK):
        near_ref[c] = jnp.full((1, CHUNK), BEYOND, jnp.float32)
    near = [near_ref[c] for c in range(WINDOW // CHUNK)]
    bounds = []
    for block in range(Q_BLOCKS):
        low, high = marks_ref[block * BLOCK], marks_ref[block * BLOCK + BLOCK - 1]
        below = sum((marks < low).astype(jnp.float32) for marks in near)
        within = sum((marks <= high).astype(jnp.float32) for marks in near)
        below = jnp.sum(below).astype(jnp.int32)
        within = jnp.sum(within).astype(jnp.int32)
        first = below // CHUNK
        bounds.append((first, ((within + CHUNK - 1) // CHUNK - first + TOGETHER - 1) // TOGETHER))
    unit(q_ref, q_hat, q_gain_ref, head_factors(squares_ref))

    scale = 1.0 / math.sqrt(HEAD_DIM)
    heads = range(q_ref.shape[1] // HEAD_DIM)
    cols = [slice(head * HEAD_DIM, head * HEAD_DIM + HEAD_DIM) for head in heads]
    for block in range(Q_BLOCKS):
        rows = slice(block * BLOCK, block * BLOCK + BLOCK)
        own = own_ref[rows, :]
        first, steps = bounds[block]

        def scores(step, tops):
            tops = list(tops)
            for c in [first + step * TOGETHER + n for n in range(TOGETHER)]:
                allowed = own == near_ref[c]
                for head in heads:
                    s = lax.dot_general(
                        q_hat[rows, cols[head]],
                        k_win[pl.ds(pl.multiple_of(c * CHUNK, CHUNK), CHUNK), cols[head]],
                        (((1,), (1,)), ((), ())),
                        preferred_element_type=jnp.float32,
                    )
                    s = jnp.where(allowed, s * scale, NEG)
                    s_ref[head, c] = s
                    for part in range(CHUNK // 128):
                        tops[head] = jnp.maximum(tops[head], s[:, part * 128 : part * 128 + 128])
            return tuple(tops)

        lowest = jnp.full((BLOCK, 128), NEG, jnp.float32)
        tops = lax.fori_loop(0, steps, scores, (lowest,) * len(heads))
        highest = [jnp.max(top, axis=1, keepdims=True) for top in tops]

        def mix(step, sums):
            sums = list(sums)
            for c in [first + step * TOGETHER + n for n in range(TOGETHER)]:
                for head in heads:
                    total, acc = sums[head]
                    e = jnp.exp(s_ref[head, c] - highest[head])
                    for part in range(CHUNK // 128):
                        total = total + e[:, part * 128 : part * 128 + 128]
                    v = v_win[pl.ds(pl.multiple_of(c * CHUNK, CHUNK), CHUNK), cols[head]]
                    acc = acc + jnp.dot(
                        e.astype(jnp.bfloat16), v, preferred_element_type=jnp.float32
                    )
                    sums[head] = (total, acc)
            return tuple(sums)

        zeros = jnp.zeros((BLOCK, 128), jnp.float32)
        sums = lax.fori_loop(0, steps, mix, ((zeros, zeros),) * len(heads))
        for head in heads:
            total, acc = sums[head]
            out_ref[rows, cols[head]] = (acc / jnp.sum(total, axis=1, keepdims=True)).astype(
                jnp.bfloat16
            )


def attend(marks, q, squares, gain, own, k_parts, far_parts, v_parts):
    width = q.shape[1]
    return pl.pallas_call(
        attend_kernel,
        out_shape=jax.ShapeDtypeStruct((ROWS, width), jnp.bfloat16),
        in_specs=[SMEM] + [VMEM] * 12,
        out_specs=VMEM,
        scratch_shapes=[
            pltpu.VMEM((ROWS, width), jnp.bfloat16),
            pltpu.VMEM((PADDED, width), jnp.bfloat16),
            pltpu.VMEM((PADDED, width), jnp.bfloat16),
            pltpu.VMEM((PADDED // CHUNK, 1, CHUNK), jnp.float32),
            pltpu.VMEM((width // HEAD_DIM, PADDED // CHUNK, BLOCK, CHUNK), jnp.float32),
        ],
        compiler_params=pltpu.CompilerParams(vmem_limit_bytes=24 << 20),
        name="attend",
    )(marks, q, squares, gain, own, *k_parts, *far_parts, *v_parts)


def on_device(tokens, ln_gain, w_query, w_key, w_value, q_gain, k_gain, seg_ids):
    width = w_query.shape[1]
    vq = jnp.concatenate([w_value, w_query], axis=1)
    vq = copies_to_all(vq, "seq", NY, OVER_Y).reshape(NY * SHARD_ROWS, 2 * width)
    vq, w_key = lax.optimization_barrier((vq, w_key))
    vq = lax.all_gather(vq, "seq", axis=0, axis_index_groups=OVER_Z, tiled=True)
    k_z = lax.all_gather(w_key, "seq", axis=0, axis_index_groups=OVER_Z)
    gain = ln_gain[None, :]
    k_z, late_tokens, seg_ids = lax.optimization_barrier((k_z, tokens, seg_ids))
    k_all = copies_to_all(k_z.reshape(NZ * SHARD_ROWS, width), "seq", NY, OVER_Y)
    k_all, moved = lax.optimization_barrier((k_all, norm(late_tokens, gain)))
    moved = in_hbm(moved)
    marks = (seg_ids + 1).astype(jnp.float32)
    mark_rows = jnp.pad(marks.reshape(-1, width), ((0, MARK_ROWS - ROWS // width), (0, 0)))

    keys, squares = project_keys(in_hbm(tokens), gain, in_hbm(k_all.reshape(D, width)))
    squares = copies_to_all(squares, "head", N_HEAD)
    k_own, k_last, k_first = unit_keys(
        keys, squares, k_gain[None, :], mark_rows.astype(jnp.bfloat16)
    )
    k_parts = (shifted(k_own, 1), k_own, shifted(k_own, -1))

    vq = in_hbm(vq)
    far = jax.ShapeDtypeStruct((2 * FAR + MARK_ROWS, width), jnp.bfloat16)
    outs = (jax.ShapeDtypeStruct((ROWS, width), jnp.bfloat16), far, far)
    v_own, far_last, far_first = project(
        values_kernel, "values", outs, width, moved, vq, k_last, k_first
    )
    far_parts = (shifted(far_last, 2), shifted(far_first, -2))
    moved, v_own = lax.optimization_barrier((moved, v_own))
    outs = (
        jax.ShapeDtypeStruct((ROWS, width), jnp.float32),
        jax.ShapeDtypeStruct((Q_BLOCKS, BLOCK), jnp.float32),
    )
    queries, squares = project(queries_kernel, "queries", outs, width, in_hbm(moved), vq)
    squares = copies_to_all(squares, "head", N_HEAD)
    v_parts = (shifted(v_own, 1), v_own, shifted(v_own, -1))
    return attend(
        marks, queries, squares, q_gain[None, :], marks[:, None], k_parts, far_parts, v_parts
    )


def solution(mesh):
    return jax.shard_map(
        on_device,
        mesh=mesh,
        in_specs=(
            P("seq", None),
            P(),
            P("seq", "head"),
            P("seq", "head"),
            P("seq", "head"),
            P("head"),
            P("head"),
            P("seq"),
        ),
        out_specs=P("seq", "head"),
        check_vma=False,
    )
```

```python
import math

import jax
import jax.numpy as jnp
from jax import lax
from jax.experimental import pallas as pl
from jax.experimental.pallas import tpu as pltpu
from jax.sharding import PartitionSpec as P

D = 3200
HEADS = 16
HEAD_DIM = 128
MOST = 1025
EPS = 1e-06
NY = 4
NZ = 16
N_SEQ = NY * NZ
N_HEAD = 8
ROWS = 768
FAR = 256
WINDOW = 2 * FAR + 3 * ROWS
OWN = FAR + ROWS
BLOCK = 256
N_BLOCKS = WINDOW // BLOCK
Q_BLOCKS = ROWS // BLOCK
CHUNK = 256
TOGETHER = 2
PADDED = WINDOW + (TOGETHER - 1) * CHUNK
NEG = -1e30
BEYOND = 1e6
SHARD_ROWS = D // N_SEQ
MARK_ROWS = 8

OVER_Y = [[y * NZ + z for y in range(NY)] for z in range(NZ)]
OVER_Z = [[y * NZ + z for z in range(NZ)] for y in range(NY)]
VMEM = pl.BlockSpec(memory_space=pltpu.VMEM)
SMEM = pl.BlockSpec(memory_space=pltpu.SMEM)
HBM = pl.BlockSpec(memory_space=pltpu.HBM)


def copies_to_all(value, axis, size, groups=None):
    stacked = jnp.broadcast_to(value[None], (size,) + value.shape)
    return lax.all_to_all(stacked, axis, 0, 0, axis_index_groups=groups)


def shifted(value, by):
    pairs = [(i, i + by) for i in range(N_SEQ) if 0 <= i + by < N_SEQ]
    return lax.ppermute(value, "seq", pairs)


def normalised(x_ref, gain_ref):
    x = x_ref[...].astype(jnp.float32)
    mean = jnp.sum(x * x, axis=1, keepdims=True) * (1.0 / D)
    return (x * lax.rsqrt(mean + EPS) * gain_ref[...]).astype(jnp.bfloat16)


def norm_kernel(x_ref, gain_ref, out_ref, plain):
    plain[...] = normalised(x_ref, gain_ref)
    for z in range(NZ):
        for y in range(NY):
            source = (y * NZ + z) * SHARD_ROWS
            target = (z * NY + y) * SHARD_ROWS
            out_ref[:, target : target + SHARD_ROWS] = plain[:, source : source + SHARD_ROWS]


def norm(tokens, gain):
    rows = 128
    block = pl.BlockSpec((rows, D), lambda i: (i, 0))
    return pl.pallas_call(
        norm_kernel,
        out_shape=jax.ShapeDtypeStruct((ROWS, D), jnp.bfloat16),
        grid=(ROWS // rows,),
        in_specs=[block, pl.BlockSpec((1, D), lambda i: (0, 0))],
        out_specs=block,
        scratch_shapes=[pltpu.VMEM((rows, D), jnp.bfloat16)],
        compiler_params=pltpu.CompilerParams(vmem_limit_bytes=10 << 20),
        name="norm",
    )(tokens, gain)


def row_squares(values):
    sums = jnp.sum(values * values, axis=1, keepdims=True)
    return jnp.transpose(jnp.broadcast_to(sums, (BLOCK, 128)))[:1]


def loads_of(x_ref, x, sem):
    loads = []
    for block in range(Q_BLOCKS):
        rows = pl.ds(block * BLOCK, BLOCK)
        loads.append(pltpu.make_async_copy(x_ref.at[rows], x.at[rows], sem.at[block]))
    return loads


def loaded_blocks(x_ref, w_ref, at, x, w, sem):
    load_w = pltpu.make_async_copy(w_ref.at[:, pl.ds(at, w.shape[1])], w, sem.at[Q_BLOCKS])
    loads = loads_of(x_ref, x, sem)
    for load in (load_w, *loads):
        load.start()
    load_w.wait()
    for block in range(Q_BLOCKS):
        loads[block].wait()
        rows = slice(block * BLOCK, block * BLOCK + BLOCK)
        yield block, rows, jnp.dot(x[rows, :], w[...], preferred_element_type=jnp.float32)


def values_kernel(
    x_ref, w_ref, k_last, k_first, v_ref, last_ref, first_ref, x, w, sem
):
    last_ref[: FAR + MARK_ROWS, :] = k_last[...]
    first_ref[: FAR + MARK_ROWS, :] = k_first[...]
    for block, rows, y in loaded_blocks(x_ref, w_ref, 0, x, w, sem):
        v = y.astype(jnp.bfloat16)
        v_ref[rows, :] = v
        if block == 0:
            first_ref[FAR + MARK_ROWS :, :] = v
        if block == Q_BLOCKS - 1:
            last_ref[FAR + MARK_ROWS :, :] = v


def queries_kernel(x_ref, w_ref, q_ref, squares_ref, x, w, sem):
    for block, rows, q in loaded_blocks(x_ref, w_ref, w.shape[1], x, w, sem):
        q_ref[rows, :] = q
        squares_ref[block : block + 1, :] = row_squares(q)


def project(kernel, name, outs, width, x, w, *more):
    return pl.pallas_call(
        kernel,
        out_shape=outs,
        in_specs=[HBM, HBM] + [VMEM] * len(more),
        out_specs=(VMEM,) * len(outs),
        scratch_shapes=[
            pltpu.VMEM((ROWS, D), jnp.bfloat16),
            pltpu.VMEM((D, width), jnp.bfloat16),
            pltpu.SemaphoreType.DMA((Q_BLOCKS + 1,)),
        ],
        compiler_params=pltpu.CompilerParams(vmem_limit_bytes=16 << 20),
        name=name,
    )(x, w, *more)


def keys_kernel(x_ref, gain_ref, w_ref, k_ref, squares_ref, x, w, sem):
    load_w = pltpu.make_async_copy(w_ref, w, sem.at[Q_BLOCKS])
    loads = loads_of(x_ref, x, sem)
    for load in (loads[0], load_w, *loads[1:]):
        load.start()
    for block in range(Q_BLOCKS):
        rows = slice(block * BLOCK, block * BLOCK + BLOCK)
        loads[block].wait()
        normed = normalised(x.at[rows, :], gain_ref)
        if block == 0:
            load_w.wait()
        k = jnp.dot(normed, w[...], preferred_element_type=jnp.float32)
        k_ref[rows, :] = k
        squares_ref[block : block + 1, :] = row_squares(k)


def project_keys(tokens, gain, w):
    width = w.shape[1]
    return pl.pallas_call(
        keys_kernel,
        out_shape=(
            jax.ShapeDtypeStruct((ROWS, width), jnp.float32),
            jax.ShapeDtypeStruct((Q_BLOCKS, BLOCK), jnp.float32),
        ),
        in_specs=[HBM, VMEM, HBM],
        out_specs=(VMEM,) * 2,
        scratch_shapes=[
            pltpu.VMEM((ROWS, D), jnp.bfloat16),
            pltpu.VMEM((D, width), jnp.bfloat16),
            pltpu.SemaphoreType.DMA((Q_BLOCKS + 1,)),
        ],
        compiler_params=pltpu.CompilerParams(vmem_limit_bytes=20 << 20),
        name="keys",
    )(tokens, gain, w)


def in_hbm(value):
    return pltpu.with_memory_space_constraint(value, pltpu.HBM)


def head_factors(squares_ref):
    total = squares_ref[0]
    for device in range(1, N_HEAD):
        total = total + squares_ref[device]
    return lax.rsqrt(total / (HEADS * HEAD_DIM) + EPS)


def unit(source, target, gain_ref, factors):
    for block in range(Q_BLOCKS):
        factor = jnp.transpose(jnp.broadcast_to(factors[block : block + 1], (128, BLOCK)))
        rows = slice(block * BLOCK, block * BLOCK + BLOCK)
        for start in range(0, source.shape[1], HEAD_DIM):
            cols = slice(start, start + HEAD_DIM)
            target[rows, cols] = (source[rows, cols] * factor * gain_ref[:, cols]).astype(
                jnp.bfloat16
            )


def unit_keys_kernel(k_ref, squares_ref, gain_ref, marks_ref, out_ref, last_ref, first_ref):
    unit(k_ref, out_ref, gain_ref, head_factors(squares_ref))
    out_ref[ROWS:, :] = marks_ref[...]
    last_ref[:FAR, :] = out_ref[ROWS - FAR : ROWS, :]
    first_ref[:FAR, :] = out_ref[:FAR, :]
    spare = jnp.zeros((MARK_ROWS - 1, out_ref.shape[1]), jnp.float32)
    marks = marks_ref[...].astype(jnp.float32)
    last_ref[FAR:, :] = jnp.concatenate([marks[Q_BLOCKS - 1 : Q_BLOCKS], spare]).astype(jnp.bfloat16)
    first_ref[FAR:, :] = jnp.concatenate([marks[:1], spare]).astype(jnp.bfloat16)


def unit_keys(k, squares, gain, marks):
    width = k.shape[1]
    far = jax.ShapeDtypeStruct((FAR + MARK_ROWS, width), jnp.bfloat16)
    return pl.pallas_call(
        unit_keys_kernel,
        out_shape=(jax.ShapeDtypeStruct((ROWS + MARK_ROWS, width), jnp.bfloat16), far, far),
        in_specs=[VMEM] * 4,
        out_specs=(VMEM,) * 3,
        compiler_params=pltpu.CompilerParams(vmem_limit_bytes=8 << 20),
        name="unit_keys",
    )(k, squares, gain, marks)


def attend_kernel(
    marks_ref, q_ref, squares_ref, q_gain_ref, own_ref, kb, kc, kd, far_a, far_e, vb, vc, vd,
    out_ref, q_hat, k_win, v_win, near_ref, s_ref,
):
    start = 0
    for k_part, v_part in ((far_a, None), (kb, vb), (kc, vc), (kd, vd), (far_e, None)):
        rows = FAR if v_part is None else ROWS
        k_win[start : start + rows, :] = k_part[:rows, :]
        if v_part is None:
            v_win[start : start + rows, :] = k_part[rows + MARK_ROWS :, :]
        else:
            v_win[start : start + rows, :] = v_part[...]
        marks = k_part[rows : rows + MARK_ROWS, :].astype(jnp.float32)
        if start > OWN:
            marks = jnp.where(marks == 0, BEYOND, marks)
        for n in range(rows // CHUNK):
            near_ref[start // CHUNK + n] = marks[n : n + 1]
        start += rows
    k_win[WINDOW:, :] = jnp.zeros((PADDED - WINDOW, k_win.shape[1]), jnp.bfloat16)
    v_win[WINDOW:, :] = jnp.zeros((PADDED - WINDOW, v_win.shape[1]), jnp.bfloat16)
    for c in range(WINDOW // CHUNK, PADDED // CHUNK):
        near_ref[c] = jnp.full((1, CHUNK), BEYOND, jnp.float32)
    near = [near_ref[c] for c in range(WINDOW // CHUNK)]
    bounds = []
    for block in range(Q_BLOCKS):
        low, high = marks_ref[block * BLOCK], marks_ref[block * BLOCK + BLOCK - 1]
        below = sum((marks < low).astype(jnp.float32) for marks in near)
        within = sum((marks <= high).astype(jnp.float32) for marks in near)
        below = jnp.sum(below).astype(jnp.int32)
        within = jnp.sum(within).astype(jnp.int32)
        first = below // CHUNK
        bounds.append((first, ((within + CHUNK - 1) // CHUNK - first + TOGETHER - 1) // TOGETHER))
    unit(q_ref, q_hat, q_gain_ref, head_factors(squares_ref))

    scale = 1.0 / math.sqrt(HEAD_DIM)
    heads = range(q_ref.shape[1] // HEAD_DIM)
    cols = [slice(head * HEAD_DIM, head * HEAD_DIM + HEAD_DIM) for head in heads]
    for block in range(Q_BLOCKS):
        rows = slice(block * BLOCK, block * BLOCK + BLOCK)
        own = own_ref[rows, :]
        first, steps = bounds[block]

        def scores(step, tops):
            tops = list(tops)
            for c in [first + step * TOGETHER + n for n in range(TOGETHER)]:
                allowed = own == near_ref[c]
                for head in heads:
                    s = lax.dot_general(
                        q_hat[rows, cols[head]],
                        k_win[pl.ds(pl.multiple_of(c * CHUNK, CHUNK), CHUNK), cols[head]],
                        (((1,), (1,)), ((), ())),
                        preferred_element_type=jnp.float32,
                    )
                    s = jnp.where(allowed, s * scale, NEG)
                    s_ref[head, c] = s
                    for part in range(CHUNK // 128):
                        tops[head] = jnp.maximum(tops[head], s[:, part * 128 : part * 128 + 128])
            return tuple(tops)

        lowest = jnp.full((BLOCK, 128), NEG, jnp.float32)
        tops = lax.fori_loop(0, steps, scores, (lowest,) * len(heads))
        highest = [jnp.max(top, axis=1, keepdims=True) for top in tops]

        def expos(step, totals):
            totals = list(totals)
            for c in [first + step * TOGETHER + n for n in range(TOGETHER)]:
                for head in heads:
                    e = jnp.exp(s_ref[head, c] - highest[head])
                    s_ref[head, c] = e
                    for part in range(CHUNK // 128):
                        totals[head] = totals[head] + e[:, part * 128 : part * 128 + 128]
            return tuple(totals)

        zeros = jnp.zeros((BLOCK, 128), jnp.float32)
        totals = lax.fori_loop(0, steps, expos, (zeros,) * len(heads))
        inverse = [1.0 / jnp.sum(total, axis=1, keepdims=True) for total in totals]

        def mix(step, accs):
            accs = list(accs)
            for c in [first + step * TOGETHER + n for n in range(TOGETHER)]:
                for head in heads:
                    w = (s_ref[head, c] * inverse[head]).astype(jnp.bfloat16)
                    v = v_win[pl.ds(pl.multiple_of(c * CHUNK, CHUNK), CHUNK), cols[head]]
                    accs[head] = accs[head] + jnp.dot(w, v, preferred_element_type=jnp.float32)
            return tuple(accs)

        accs = lax.fori_loop(0, steps, mix, (zeros,) * len(heads))
        for head in heads:
            out_ref[rows, cols[head]] = accs[head].astype(jnp.bfloat16)


def attend(marks, q, squares, gain, own, k_parts, far_parts, v_parts):
    width = q.shape[1]
    return pl.pallas_call(
        attend_kernel,
        out_shape=jax.ShapeDtypeStruct((ROWS, width), jnp.bfloat16),
        in_specs=[SMEM] + [VMEM] * 12,
        out_specs=VMEM,
        scratch_shapes=[
            pltpu.VMEM((ROWS, width), jnp.bfloat16),
            pltpu.VMEM((PADDED, width), jnp.bfloat16),
            pltpu.VMEM((PADDED, width), jnp.bfloat16),
            pltpu.VMEM((PADDED // CHUNK, 1, CHUNK), jnp.float32),
            pltpu.VMEM((width // HEAD_DIM, PADDED // CHUNK, BLOCK, CHUNK), jnp.float32),
        ],
        compiler_params=pltpu.CompilerParams(vmem_limit_bytes=24 << 20),
        name="attend",
    )(marks, q, squares, gain, own, *k_parts, *far_parts, *v_parts)


def on_device(tokens, ln_gain, w_query, w_key, w_value, q_gain, k_gain, seg_ids):
    width = w_query.shape[1]
    vq = jnp.concatenate([w_value, w_query], axis=1)
    vq = copies_to_all(vq, "seq", NY, OVER_Y).reshape(NY * SHARD_ROWS, 2 * width)
    vq, w_key = lax.optimization_barrier((vq, w_key))
    vq = lax.all_gather(vq, "seq", axis=0, axis_index_groups=OVER_Z, tiled=True)
    k_z = lax.all_gather(w_key, "seq", axis=0, axis_index_groups=OVER_Z)
    gain = ln_gain[None, :]
    k_z, late_tokens, seg_ids = lax.optimization_barrier((k_z, tokens, seg_ids))
    k_all = copies_to_all(k_z.reshape(NZ * SHARD_ROWS, width), "seq", NY, OVER_Y)
    k_all, moved = lax.optimization_barrier((k_all, norm(late_tokens, gain)))
    moved = in_hbm(moved)
    marks = (seg_ids + 1).astype(jnp.float32)
    mark_rows = jnp.pad(marks.reshape(-1, width), ((0, MARK_ROWS - ROWS // width), (0, 0)))

    keys, squares = project_keys(in_hbm(tokens), gain, in_hbm(k_all.reshape(D, width)))
    squares = copies_to_all(squares, "head", N_HEAD)
    k_own, k_last, k_first = unit_keys(
        keys, squares, k_gain[None, :], mark_rows.astype(jnp.bfloat16)
    )
    k_parts = (shifted(k_own, 1), k_own, shifted(k_own, -1))

    vq = in_hbm(vq)
    far = jax.ShapeDtypeStruct((2 * FAR + MARK_ROWS, width), jnp.bfloat16)
    outs = (jax.ShapeDtypeStruct((ROWS, width), jnp.bfloat16), far, far)
    v_own, far_last, far_first = project(
        values_kernel, "values", outs, width, moved, vq, k_last, k_first
    )
    far_parts = (shifted(far_last, 2), shifted(far_first, -2))
    moved, v_own = lax.optimization_barrier((moved, v_own))
    outs = (
        jax.ShapeDtypeStruct((ROWS, width), jnp.float32),
        jax.ShapeDtypeStruct((Q_BLOCKS, BLOCK), jnp.float32),
    )
    queries, squares = project(queries_kernel, "queries", outs, width, in_hbm(moved), vq)
    squares = copies_to_all(squares, "head", N_HEAD)
    v_parts = (shifted(v_own, 1), v_own, shifted(v_own, -1))
    return attend(
        marks, queries, squares, q_gain[None, :], marks[:, None], k_parts, far_parts, v_parts
    )


def solution(mesh):
    return jax.shard_map(
        on_device,
        mesh=mesh,
        in_specs=(
            P("seq", None),
            P(),
            P("seq", "head"),
            P("seq", "head"),
            P("seq", "head"),
            P("head"),
            P("head"),
            P("seq"),
        ),
        out_specs=P("seq", "head"),
        check_vma=False,
    )
```

```python
import math

import jax
import jax.numpy as jnp
from jax import lax
from jax.experimental import pallas as pl
from jax.experimental.pallas import tpu as pltpu
from jax.sharding import PartitionSpec as P

D = 3200
HEADS = 16
HEAD_DIM = 128
MOST = 1025
EPS = 1e-06
NY = 4
NZ = 16
N_SEQ = NY * NZ
N_HEAD = 8
ROWS = 768
FAR = 256
WINDOW = 2 * FAR + 3 * ROWS
OWN = FAR + ROWS
BLOCK = 256
N_BLOCKS = WINDOW // BLOCK
Q_BLOCKS = ROWS // BLOCK
CHUNK = 256
TOGETHER = 3
PADDED = WINDOW + (TOGETHER - 1) * CHUNK
NEG = -1e30
BEYOND = 1e6
SHARD_ROWS = D // N_SEQ
MARK_ROWS = 8

OVER_Y = [[y * NZ + z for y in range(NY)] for z in range(NZ)]
OVER_Z = [[y * NZ + z for z in range(NZ)] for y in range(NY)]
VMEM = pl.BlockSpec(memory_space=pltpu.VMEM)
SMEM = pl.BlockSpec(memory_space=pltpu.SMEM)
HBM = pl.BlockSpec(memory_space=pltpu.HBM)


def copies_to_all(value, axis, size, groups=None):
    stacked = jnp.broadcast_to(value[None], (size,) + value.shape)
    return lax.all_to_all(stacked, axis, 0, 0, axis_index_groups=groups)


def shifted(value, by):
    pairs = [(i, i + by) for i in range(N_SEQ) if 0 <= i + by < N_SEQ]
    return lax.ppermute(value, "seq", pairs)


def normalised(x_ref, gain_ref):
    x = x_ref[...].astype(jnp.float32)
    mean = jnp.sum(x * x, axis=1, keepdims=True) * (1.0 / D)
    return (x * lax.rsqrt(mean + EPS) * gain_ref[...]).astype(jnp.bfloat16)


def norm_kernel(x_ref, gain_ref, out_ref, plain):
    plain[...] = normalised(x_ref, gain_ref)
    for z in range(NZ):
        for y in range(NY):
            source = (y * NZ + z) * SHARD_ROWS
            target = (z * NY + y) * SHARD_ROWS
            out_ref[:, target : target + SHARD_ROWS] = plain[:, source : source + SHARD_ROWS]


def norm(tokens, gain):
    rows = 128
    block = pl.BlockSpec((rows, D), lambda i: (i, 0))
    return pl.pallas_call(
        norm_kernel,
        out_shape=jax.ShapeDtypeStruct((ROWS, D), jnp.bfloat16),
        grid=(ROWS // rows,),
        in_specs=[block, pl.BlockSpec((1, D), lambda i: (0, 0))],
        out_specs=block,
        scratch_shapes=[pltpu.VMEM((rows, D), jnp.bfloat16)],
        compiler_params=pltpu.CompilerParams(vmem_limit_bytes=10 << 20),
        name="norm",
    )(tokens, gain)


def row_squares(values):
    sums = jnp.sum(values * values, axis=1, keepdims=True)
    return jnp.transpose(jnp.broadcast_to(sums, (BLOCK, 128)))[:1]


def loads_of(x_ref, x, sem):
    loads = []
    for block in range(Q_BLOCKS):
        rows = pl.ds(block * BLOCK, BLOCK)
        loads.append(pltpu.make_async_copy(x_ref.at[rows], x.at[rows], sem.at[block]))
    return loads


def loaded_blocks(x_ref, w_ref, at, x, w, sem):
    load_w = pltpu.make_async_copy(w_ref.at[:, pl.ds(at, w.shape[1])], w, sem.at[Q_BLOCKS])
    loads = loads_of(x_ref, x, sem)
    for load in (load_w, *loads):
        load.start()
    load_w.wait()
    for block in range(Q_BLOCKS):
        loads[block].wait()
        rows = slice(block * BLOCK, block * BLOCK + BLOCK)
        yield block, rows, jnp.dot(x[rows, :], w[...], preferred_element_type=jnp.float32)


def values_kernel(
    x_ref, w_ref, k_last, k_first, v_ref, last_ref, first_ref, x, w, sem
):
    last_ref[: FAR + MARK_ROWS, :] = k_last[...]
    first_ref[: FAR + MARK_ROWS, :] = k_first[...]
    for block, rows, y in loaded_blocks(x_ref, w_ref, 0, x, w, sem):
        v = y.astype(jnp.bfloat16)
        v_ref[rows, :] = v
        if block == 0:
            first_ref[FAR + MARK_ROWS :, :] = v
        if block == Q_BLOCKS - 1:
            last_ref[FAR + MARK_ROWS :, :] = v


def queries_kernel(x_ref, w_ref, q_ref, squares_ref, x, w, sem):
    for block, rows, q in loaded_blocks(x_ref, w_ref, w.shape[1], x, w, sem):
        q_ref[rows, :] = q
        squares_ref[block : block + 1, :] = row_squares(q)


def project(kernel, name, outs, width, x, w, *more):
    return pl.pallas_call(
        kernel,
        out_shape=outs,
        in_specs=[HBM, HBM] + [VMEM] * len(more),
        out_specs=(VMEM,) * len(outs),
        scratch_shapes=[
            pltpu.VMEM((ROWS, D), jnp.bfloat16),
            pltpu.VMEM((D, width), jnp.bfloat16),
            pltpu.SemaphoreType.DMA((Q_BLOCKS + 1,)),
        ],
        compiler_params=pltpu.CompilerParams(vmem_limit_bytes=16 << 20),
        name=name,
    )(x, w, *more)


def keys_kernel(x_ref, gain_ref, w_ref, k_ref, squares_ref, x, w, sem):
    load_w = pltpu.make_async_copy(w_ref, w, sem.at[Q_BLOCKS])
    loads = loads_of(x_ref, x, sem)
    for load in (loads[0], load_w, *loads[1:]):
        load.start()
    for block in range(Q_BLOCKS):
        rows = slice(block * BLOCK, block * BLOCK + BLOCK)
        loads[block].wait()
        normed = normalised(x.at[rows, :], gain_ref)
        if block == 0:
            load_w.wait()
        k = jnp.dot(normed, w[...], preferred_element_type=jnp.float32)
        k_ref[rows, :] = k
        squares_ref[block : block + 1, :] = row_squares(k)


def project_keys(tokens, gain, w):
    width = w.shape[1]
    return pl.pallas_call(
        keys_kernel,
        out_shape=(
            jax.ShapeDtypeStruct((ROWS, width), jnp.float32),
            jax.ShapeDtypeStruct((Q_BLOCKS, BLOCK), jnp.float32),
        ),
        in_specs=[HBM, VMEM, HBM],
        out_specs=(VMEM,) * 2,
        scratch_shapes=[
            pltpu.VMEM((ROWS, D), jnp.bfloat16),
            pltpu.VMEM((D, width), jnp.bfloat16),
            pltpu.SemaphoreType.DMA((Q_BLOCKS + 1,)),
        ],
        compiler_params=pltpu.CompilerParams(vmem_limit_bytes=20 << 20),
        name="keys",
    )(tokens, gain, w)


def in_hbm(value):
    return pltpu.with_memory_space_constraint(value, pltpu.HBM)


def head_factors(squares_ref):
    total = squares_ref[0]
    for device in range(1, N_HEAD):
        total = total + squares_ref[device]
    return lax.rsqrt(total / (HEADS * HEAD_DIM) + EPS)


def unit(source, target, gain_ref, factors):
    for block in range(Q_BLOCKS):
        factor = jnp.transpose(jnp.broadcast_to(factors[block : block + 1], (128, BLOCK)))
        rows = slice(block * BLOCK, block * BLOCK + BLOCK)
        for start in range(0, source.shape[1], HEAD_DIM):
            cols = slice(start, start + HEAD_DIM)
            target[rows, cols] = (source[rows, cols] * factor * gain_ref[:, cols]).astype(
                jnp.bfloat16
            )


def unit_keys_kernel(k_ref, squares_ref, gain_ref, marks_ref, out_ref, last_ref, first_ref):
    unit(k_ref, out_ref, gain_ref, head_factors(squares_ref))
    out_ref[ROWS:, :] = marks_ref[...]
    last_ref[:FAR, :] = out_ref[ROWS - FAR : ROWS, :]
    first_ref[:FAR, :] = out_ref[:FAR, :]
    spare = jnp.zeros((MARK_ROWS - 1, out_ref.shape[1]), jnp.float32)
    marks = marks_ref[...].astype(jnp.float32)
    last_ref[FAR:, :] = jnp.concatenate([marks[Q_BLOCKS - 1 : Q_BLOCKS], spare]).astype(jnp.bfloat16)
    first_ref[FAR:, :] = jnp.concatenate([marks[:1], spare]).astype(jnp.bfloat16)


def unit_keys(k, squares, gain, marks):
    width = k.shape[1]
    far = jax.ShapeDtypeStruct((FAR + MARK_ROWS, width), jnp.bfloat16)
    return pl.pallas_call(
        unit_keys_kernel,
        out_shape=(jax.ShapeDtypeStruct((ROWS + MARK_ROWS, width), jnp.bfloat16), far, far),
        in_specs=[VMEM] * 4,
        out_specs=(VMEM,) * 3,
        compiler_params=pltpu.CompilerParams(vmem_limit_bytes=8 << 20),
        name="unit_keys",
    )(k, squares, gain, marks)


def attend_kernel(
    marks_ref, q_ref, squares_ref, q_gain_ref, own_ref, kb, kc, kd, far_a, far_e, vb, vc, vd,
    out_ref, q_hat, k_win, v_win, near_ref, s_ref,
):
    start = 0
    for k_part, v_part in ((far_a, None), (kb, vb), (kc, vc), (kd, vd), (far_e, None)):
        rows = FAR if v_part is None else ROWS
        k_win[start : start + rows, :] = k_part[:rows, :]
        if v_part is None:
            v_win[start : start + rows, :] = k_part[rows + MARK_ROWS :, :]
        else:
            v_win[start : start + rows, :] = v_part[...]
        marks = k_part[rows : rows + MARK_ROWS, :].astype(jnp.float32)
        if start > OWN:
            marks = jnp.where(marks == 0, BEYOND, marks)
        for n in range(rows // CHUNK):
            near_ref[start // CHUNK + n] = marks[n : n + 1]
        start += rows
    k_win[WINDOW:, :] = jnp.zeros((PADDED - WINDOW, k_win.shape[1]), jnp.bfloat16)
    v_win[WINDOW:, :] = jnp.zeros((PADDED - WINDOW, v_win.shape[1]), jnp.bfloat16)
    for c in range(WINDOW // CHUNK, PADDED // CHUNK):
        near_ref[c] = jnp.full((1, CHUNK), BEYOND, jnp.float32)
    near = [near_ref[c] for c in range(WINDOW // CHUNK)]
    bounds = []
    for block in range(Q_BLOCKS):
        low, high = marks_ref[block * BLOCK], marks_ref[block * BLOCK + BLOCK - 1]
        below = sum((marks < low).astype(jnp.float32) for marks in near)
        within = sum((marks <= high).astype(jnp.float32) for marks in near)
        below = jnp.sum(below).astype(jnp.int32)
        within = jnp.sum(within).astype(jnp.int32)
        first = below // CHUNK
        bounds.append((first, ((within + CHUNK - 1) // CHUNK - first + TOGETHER - 1) // TOGETHER))
    unit(q_ref, q_hat, q_gain_ref, head_factors(squares_ref))

    scale = 1.0 / math.sqrt(HEAD_DIM)
    heads = range(q_ref.shape[1] // HEAD_DIM)
    cols = [slice(head * HEAD_DIM, head * HEAD_DIM + HEAD_DIM) for head in heads]
    for block in range(Q_BLOCKS):
        rows = slice(block * BLOCK, block * BLOCK + BLOCK)
        own = own_ref[rows, :]
        first, steps = bounds[block]

        def scores(step, tops):
            tops = list(tops)
            for c in [first + step * TOGETHER + n for n in range(TOGETHER)]:
                allowed = own == near_ref[c]
                for head in heads:
                    s = lax.dot_general(
                        q_hat[rows, cols[head]],
                        k_win[pl.ds(pl.multiple_of(c * CHUNK, CHUNK), CHUNK), cols[head]],
                        (((1,), (1,)), ((), ())),
                        preferred_element_type=jnp.float32,
                    )
                    s = jnp.where(allowed, s * scale, NEG)
                    s_ref[head, c] = s
                    for part in range(CHUNK // 128):
                        tops[head] = jnp.maximum(tops[head], s[:, part * 128 : part * 128 + 128])
            return tuple(tops)

        lowest = jnp.full((BLOCK, 128), NEG, jnp.float32)
        tops = lax.fori_loop(0, steps, scores, (lowest,) * len(heads))
        highest = [jnp.max(top, axis=1, keepdims=True) for top in tops]

        def expos(step, totals):
            totals = list(totals)
            for c in [first + step * TOGETHER + n for n in range(TOGETHER)]:
                for head in heads:
                    e = jnp.exp(s_ref[head, c] - highest[head])
                    s_ref[head, c] = e
                    for part in range(CHUNK // 128):
                        totals[head] = totals[head] + e[:, part * 128 : part * 128 + 128]
            return tuple(totals)

        zeros = jnp.zeros((BLOCK, 128), jnp.float32)
        totals = lax.fori_loop(0, steps, expos, (zeros,) * len(heads))
        inverse = [1.0 / jnp.sum(total, axis=1, keepdims=True) for total in totals]

        def mix(step, accs):
            accs = list(accs)
            for c in [first + step * TOGETHER + n for n in range(TOGETHER)]:
                for head in heads:
                    w = (s_ref[head, c] * inverse[head]).astype(jnp.bfloat16)
                    v = v_win[pl.ds(pl.multiple_of(c * CHUNK, CHUNK), CHUNK), cols[head]]
                    accs[head] = accs[head] + jnp.dot(w, v, preferred_element_type=jnp.float32)
            return tuple(accs)

        accs = lax.fori_loop(0, steps, mix, (zeros,) * len(heads))
        for head in heads:
            out_ref[rows, cols[head]] = accs[head].astype(jnp.bfloat16)


def attend(marks, q, squares, gain, own, k_parts, far_parts, v_parts):
    width = q.shape[1]
    return pl.pallas_call(
        attend_kernel,
        out_shape=jax.ShapeDtypeStruct((ROWS, width), jnp.bfloat16),
        in_specs=[SMEM] + [VMEM] * 12,
        out_specs=VMEM,
        scratch_shapes=[
            pltpu.VMEM((ROWS, width), jnp.bfloat16),
            pltpu.VMEM((PADDED, width), jnp.bfloat16),
            pltpu.VMEM((PADDED, width), jnp.bfloat16),
            pltpu.VMEM((PADDED // CHUNK, 1, CHUNK), jnp.float32),
            pltpu.VMEM((width // HEAD_DIM, PADDED // CHUNK, BLOCK, CHUNK), jnp.float32),
        ],
        compiler_params=pltpu.CompilerParams(vmem_limit_bytes=24 << 20),
        name="attend",
    )(marks, q, squares, gain, own, *k_parts, *far_parts, *v_parts)


def on_device(tokens, ln_gain, w_query, w_key, w_value, q_gain, k_gain, seg_ids):
    width = w_query.shape[1]
    vq = jnp.concatenate([w_value, w_query], axis=1)
    vq = copies_to_all(vq, "seq", NY, OVER_Y).reshape(NY * SHARD_ROWS, 2 * width)
    vq, w_key = lax.optimization_barrier((vq, w_key))
    vq = lax.all_gather(vq, "seq", axis=0, axis_index_groups=OVER_Z, tiled=True)
    k_z = lax.all_gather(w_key, "seq", axis=0, axis_index_groups=OVER_Z)
    gain = ln_gain[None, :]
    k_z, late_tokens, seg_ids = lax.optimization_barrier((k_z, tokens, seg_ids))
    k_all = copies_to_all(k_z.reshape(NZ * SHARD_ROWS, width), "seq", NY, OVER_Y)
    k_all, moved = lax.optimization_barrier((k_all, norm(late_tokens, gain)))
    moved = in_hbm(moved)
    marks = (seg_ids + 1).astype(jnp.float32)
    mark_rows = jnp.pad(marks.reshape(-1, width), ((0, MARK_ROWS - ROWS // width), (0, 0)))

    keys, squares = project_keys(in_hbm(tokens), gain, in_hbm(k_all.reshape(D, width)))
    squares = copies_to_all(squares, "head", N_HEAD)
    k_own, k_last, k_first = unit_keys(
        keys, squares, k_gain[None, :], mark_rows.astype(jnp.bfloat16)
    )
    k_parts = (shifted(k_own, 1), k_own, shifted(k_own, -1))

    vq = in_hbm(vq)
    far = jax.ShapeDtypeStruct((2 * FAR + MARK_ROWS, width), jnp.bfloat16)
    outs = (jax.ShapeDtypeStruct((ROWS, width), jnp.bfloat16), far, far)
    v_own, far_last, far_first = project(
        values_kernel, "values", outs, width, moved, vq, k_last, k_first
    )
    far_parts = (shifted(far_last, 2), shifted(far_first, -2))
    moved, v_own = lax.optimization_barrier((moved, v_own))
    outs = (
        jax.ShapeDtypeStruct((ROWS, width), jnp.float32),
        jax.ShapeDtypeStruct((Q_BLOCKS, BLOCK), jnp.float32),
    )
    queries, squares = project(queries_kernel, "queries", outs, width, in_hbm(moved), vq)
    squares = copies_to_all(squares, "head", N_HEAD)
    v_parts = (shifted(v_own, 1), v_own, shifted(v_own, -1))
    return attend(
        marks, queries, squares, q_gain[None, :], marks[:, None], k_parts, far_parts, v_parts
    )


def solution(mesh):
    return jax.shard_map(
        on_device,
        mesh=mesh,
        in_specs=(
            P("seq", None),
            P(),
            P("seq", "head"),
            P("seq", "head"),
            P("seq", "head"),
            P("head"),
            P("head"),
            P("seq"),
        ),
        out_specs=P("seq", "head"),
        check_vma=False,
    )
```
